512 devices in a mesh: gx: 16 (over z_lo, x), gy: 32 (over y, z_hi, core).
Axes of the slice: x: 4, y: 8, z: 8 (z_hi: 2, z_lo: 4; z = z_hi * 4 + z_lo), core: 2. Of those that a mesh axis runs over, the one named last changes fastest.
Arguments:
- estimate: float32 [8, 2048, 4096], P(None, 'gy', 'gx'), may hold values from 0.5 to 2
- views: float32 [4, 8, 2048, 4096], P(None, None, 'gy', 'gx'), may hold values from 0.25 to 4
- psf_x: float32 [4, 15], replicated, may hold values from 0.05 to 1
- psf_y: float32 [4, 15], replicated, may hold values from 0.05 to 1
- psf_z: float32 [4, 15], replicated, may hold values from 0.05 to 1
- block_offsets: int32 [4, 2, 32, 16], replicated, may hold values from -15 to 15
- sub_shifts: int32 [4, 3, 32, 16], replicated, may hold values from 0 to 3
Outputs:
- estimate_next: float32 [8, 2048, 4096], P(None, 'gy', 'gx')
The draws below stay inside these ranges and needn't reach their ends.
All inputs are finite; a program needn't handle non-finite values.
Results may differ from the reference program's by a relative error of at most 0.0003.
Values sent between devices are 32-bit elements; how exact they have to be, the bound alone decides.
No kernel may reach another device: no remote copies, remote signals or barrier semaphores. Data moves between devices by JAX's collectives and lax.ppermute only.
A program may use at most 64 MiB of HBM per device.

```python
import math
import jax
import jax.numpy as jnp
from jax import lax

CX = 256
CY = 64
Z = 8
VIEWS = 4
TAPS = 15
HALO = 16
OFF = 15
NX = 4096
NY = 2048
BLOCK_ROWS = 32
BLOCK_COLS = 16


def with_ends(entries, key, smallest, high):
    index_at = [jax.random.randint(jax.random.fold_in(key, axis), (), 0, length) for axis, length in enumerate(entries.shape)]
    longest = entries.shape.index(max(entries.shape))
    beside = index_at[:longest] + [(index_at[longest] + 1) % entries.shape[longest]] + index_at[longest + 1:]
    return entries.at[tuple(index_at)].set(smallest).at[tuple(beside)].set(high)


def steps_of(rng, dims, cuts, low, largest):
    loudness, own = 1.0, jax.random.fold_in(rng, 6)
    for axis_at, shards_of in cuts:
        steps = jnp.exp(jax.random.uniform(jax.random.fold_in(own, axis_at), (shards_of,), jnp.float32, low / len(cuts), largest / len(cuts)))
        loudness = loudness * jnp.repeat(steps, dims[axis_at] // shards_of).reshape([-1 if axis == axis_at else 1 for axis in range(len(dims))])
    return loudness


def setup_inputs(seed: int = 0) -> dict:
    seeds = jax.random.split(jax.random.key(seed), 8)
    estimate = jnp.clip(jnp.exp(math.log(2.0) - 1.3862944 * jax.random.uniform(seeds[0], (Z, NY, NX), jnp.float32) ** steps_of(seeds[0], (Z, NY, NX), ((1, 32), (2, 16)), -0.2, 0.2)), 0.5, 2.0)
    views = jnp.clip(jnp.exp(math.log(4.0) - 2.7725887 * jax.random.uniform(seeds[1], (VIEWS, Z, NY, NX), jnp.float32) ** steps_of(seeds[1], (VIEWS, Z, NY, NX), ((2, 32), (3, 16)), -0.2, 0.2)), 0.25, 4.0)
    psf_x = jnp.clip(jnp.exp(jax.random.uniform(seeds[2], (VIEWS, TAPS), jnp.float32, math.log(0.05), math.log(1.0))), 0.05, 1.0)
    psf_y = jnp.clip(jnp.exp(jax.random.uniform(seeds[3], (VIEWS, TAPS), jnp.float32, math.log(0.05), math.log(1.0))), 0.05, 1.0)
    psf_z = jnp.clip(jnp.exp(jax.random.uniform(seeds[4], (VIEWS, TAPS), jnp.float32, math.log(0.05), math.log(1.0))), 0.05, 1.0)
    block_offsets = with_ends(jax.random.randint(seeds[5], (VIEWS, 2, BLOCK_ROWS, BLOCK_COLS), -OFF, OFF + 1), jax.random.fold_in(seeds[5], 1), -OFF, OFF).astype(jnp.int32)
    sub_shifts = with_ends(jax.random.randint(seeds[6], (VIEWS, 3, BLOCK_ROWS, BLOCK_COLS), 0, 4), jax.random.fold_in(seeds[6], 1), 0, 3).astype(jnp.int32)
    return dict(estimate=estimate, views=views, psf_x=psf_x, psf_y=psf_y, psf_z=psf_z, block_offsets=block_offsets, sub_shifts=sub_shifts)


def normalized(kernel):
    return kernel / jnp.sum(kernel, axis=-1, keepdims=True)


def blur_axis(volume, kernel, direction, flipped):
    radius = (kernel.shape[0] - 1) // 2
    kernel_taps = kernel[::-1] if flipped else kernel
    widths = [(0, 0)] * volume.ndim
    widths[direction] = (radius, radius)
    padded = jnp.pad(volume, widths)
    length = volume.shape[direction]
    running = jnp.zeros(volume.shape, jnp.float32)
    for position in range(kernel.shape[0]):
        running = running + kernel_taps[position] * lax.slice_in_dim(padded, position, position + length, axis=direction)
    return running


def blur_three(volume, kernel_cols, kernel_rows, kernel_depth, flipped):
    along_cols = blur_axis(volume, kernel_cols, 2, flipped)
    along_rows = blur_axis(along_cols, kernel_rows, 1, flipped)
    return blur_axis(along_rows, kernel_depth, 0, flipped)


def warp_view(view, offsets, shifts):
    padded = jnp.pad(view, ((0, 1), (HALO, HALO), (HALO, HALO)))
    blocks_y = offsets.shape[1]
    blocks_x = offsets.shape[2]

    def one_block(block_number):
        block_y = block_number // blocks_x
        block_x = block_number % blocks_x
        shift_x = offsets[0, block_y, block_x]
        shift_y = offsets[1, block_y, block_x]
        frac_x = shifts[0, block_y, block_x].astype(jnp.float32) / 4.0
        frac_y = shifts[1, block_y, block_x].astype(jnp.float32) / 4.0
        frac_z = shifts[2, block_y, block_x].astype(jnp.float32) / 4.0
        start_y = (block_y * CY + shift_y + HALO).astype(jnp.int32)
        start_x = (block_x * CX + shift_x + HALO).astype(jnp.int32)
        sample_box = lax.dynamic_slice(padded, (jnp.zeros((), jnp.int32), start_y, start_x), (Z + 1, CY + 1, CX + 1))
        along_x = (1.0 - frac_x) * sample_box[:, :, :-1] + frac_x * sample_box[:, :, 1:]
        along_y = (1.0 - frac_y) * along_x[:, :-1, :] + frac_y * along_x[:, 1:, :]
        return (1.0 - frac_z) * along_y[:-1] + frac_z * along_y[1:]

    pieces = lax.map(one_block, jnp.arange(blocks_y * blocks_x, dtype=jnp.int32))
    pieces = pieces.reshape(blocks_y, blocks_x, Z, CY, CX).transpose(2, 0, 3, 1, 4)
    return pieces.reshape(Z, blocks_y * CY, blocks_x * CX)


def reference(estimate, views, psf_x, psf_y, psf_z, block_offsets, sub_shifts):
    kernel_cols = normalized(psf_x)
    kernel_rows = normalized(psf_y)
    kernel_depth = normalized(psf_z)

    def add_view(view_index, running):
        warped = warp_view(views[view_index], block_offsets[view_index], sub_shifts[view_index])
        blurred = blur_three(estimate, kernel_cols[view_index], kernel_rows[view_index], kernel_depth[view_index], False)
        ratio = warped / blurred
        back = blur_three(ratio, kernel_cols[view_index], kernel_rows[view_index], kernel_depth[view_index], True)
        return running + back

    running = lax.fori_loop(0, VIEWS, add_view, jnp.zeros(estimate.shape, jnp.float32))
    return estimate * (running / VIEWS)
```

```python
import functools

import jax
import jax.numpy as jnp
from jax import lax
from jax.experimental import pallas as pl
from jax.experimental.pallas import tpu as pltpu
from jax.sharding import PartitionSpec as P

F32 = jnp.float32
BF16 = jnp.bfloat16
VIEWS = 4
TAPS = 15
Z = 8
ROWS = 64
COLS = 256
SET = 48
EDGE = 24

SMEM = pl.BlockSpec(memory_space=pltpu.SMEM)
VMEM = pl.BlockSpec(memory_space=pltpu.VMEM)


def iota(shape, dim):
    return lax.broadcasted_iota(jnp.int32, shape, dim)


def sample_row(inner, idx):
    if inner:
        return idx + 8
    return jnp.where(
        idx < 8, idx, jnp.where(idx < 16, idx + 48, jnp.where(idx < 32, idx - 32, idx + 32))
    )


def estimate_row(inner, idx):
    return idx if inner else jnp.where(idx < 40, idx - 24, idx + 8)


def output_row(inner, idx):
    return idx if inner else jnp.where(idx < 64, idx, jnp.where(idx < 88, idx - 88, idx - 24))


def estimate_rows(inner):
    return 64 if inner else 80


def output_rows(inner):
    return 64 if inner else 112


def strip_col(lane):
    return jnp.where(lane < 8, lane - 8, jnp.where(lane < 16, lane + 248, 4096))


def split(value):
    high = value.astype(BF16)
    return high, (value - high.astype(F32)).astype(BF16)


def band(k_ref, base, differ):
    total = jnp.zeros(differ.shape, F32)
    for tap in range(TAPS):
        total = jnp.where(differ == tap, k_ref[base + tap], total)
    return total


def matrices_kernel(k_ref, ly_i, ly_o, f_hi, f_lo, f_t, f_s, b_hi, b_lo, b_t, m_i, n_i, m_o, n_o):
    kx, ky = 0, VIEWS * TAPS
    for inner, ly in ((True, ly_i), (False, ly_o)):
        count = estimate_rows(inner)
        shape = (SET, 3 * count)
        lane = iota(shape, 1)
        seg = jnp.where(lane < count, 0, jnp.where(lane < 2 * count, 1, 2))
        differ = estimate_row(inner, lane - seg * count) - sample_row(inner, iota(shape, 0)) + 7
        for v in range(VIEWS):
            weight = band(k_ref, ky + v * TAPS, differ)
            high = weight.astype(BF16).astype(F32)
            ly[v * SET : (v + 1) * SET, :] = jnp.where(seg < 2, high, weight - high).astype(BF16)

    for inner, m_ref, n_ref in ((True, m_i, n_i), (False, m_o, n_o)):
        shape = (output_rows(inner), VIEWS * SET)
        lane = iota(shape, 1)
        view = lane // SET
        differ = output_row(inner, iota(shape, 0)) - sample_row(inner, lane - view * SET) + 7
        weight = jnp.zeros(shape, F32)
        for v in range(VIEWS):
            weight = jnp.where(view == v, band(k_ref, ky + v * TAPS, differ), weight)
        high, low = split(weight)
        m_ref[...] = high
        n_ref[...] = low

    def per_view(v, carry):
        base = kx + v * TAPS
        differ = iota((COLS, COLS), 0) - iota((COLS, COLS), 1) + 7
        high, low = split(band(k_ref, base, differ))
        f_hi[v] = high
        f_lo[v] = low
        high, low = split(band(k_ref, base, 14 - differ))
        b_hi[v] = high
        b_lo[v] = low
        for out_ref, width in ((f_t, COLS), (f_s, 128)):
            shape = (256, width)
            row = iota(shape, 0)
            second = row >= 128
            h = jnp.where(second, row - 128, row)
            place = jnp.where(h < 48, h, h - 48)
            source = jnp.where(
                place < 16,
                place - 16,
                jnp.where(place < 32, place + 240, jnp.where(place < 40, place - 32, place + 208)),
            )
            limit = 32 if width == COLS else 48
            good = (place < limit) & (h < jnp.where(second, 48, 96))
            target = iota(shape, 1) if width == COLS else strip_col(iota(shape, 1))
            weight = band(k_ref, base, jnp.where(good, source - target + 7, -1))
            high = weight.astype(BF16).astype(F32)
            out_ref[v] = jnp.where(second, weight - high, high).astype(BF16)
        shape = (128, COLS)
        row = iota(shape, 0)
        seg = row // 16
        differ = iota(shape, 1) - strip_col(row - seg * 16) + 7
        weight = band(k_ref, base, jnp.where(seg < 3, differ, -1))
        high = weight.astype(BF16).astype(F32)
        b_t[v] = jnp.where(seg < 2, high, weight - high).astype(BF16)
        return carry

    lax.fori_loop(0, VIEWS, per_view, 0)


def matrices(kernels):
    shapes = [
        (192, 192), (192, 240), (4, 256, 256), (4, 256, 256), (4, 256, 256), (4, 256, 128),
        (4, 256, 256), (4, 256, 256), (4, 128, 256), (64, 192), (64, 192), (112, 192), (112, 192),
    ]
    return pl.pallas_call(
        matrices_kernel,
        out_shape=[jax.ShapeDtypeStruct(s, BF16) for s in shapes],
        in_specs=[SMEM],
        out_specs=[VMEM] * len(shapes),
        name="matrices",
        cost_estimate=pl.CostEstimate(flops=8_000_000, bytes_accessed=4_000_000, transcendentals=0),
    )(kernels)


def pack_estimate_kernel(e_ref, left_ref, right_ref):
    lane = iota((ROWS, 128), 1) // 16
    left = jnp.zeros((ROWS, 128), F32)
    right = jnp.zeros((ROWS, 128), F32)
    for z in range(Z):
        a = pltpu.roll(e_ref[z, :, 0:128], z * 16, 1) if z else e_ref[z, :, 0:128]
        b = pltpu.roll(e_ref[z, :, 128:256], (z * 16 + 16) % 128, 1) if z < 7 else e_ref[z, :, 128:256]
        left = jnp.where(lane == z, a, left)
        right = jnp.where(lane == z, b, right)
    left_ref[...] = left
    right_ref[...] = right


def pack_estimate(estimate):
    return pl.pallas_call(
        pack_estimate_kernel,
        out_shape=[jax.ShapeDtypeStruct((ROWS, 128), F32)] * 2,
        in_specs=[VMEM],
        out_specs=[VMEM] * 2,
        name="pack_estimate",
    )(estimate)


def pack_views_kernel(v_ref, left_ref, right_ref):
    lane = iota((ROWS, 128), 1) // 24
    for v in range(VIEWS):
        for half in range(2):
            left = jnp.zeros((ROWS, 128), F32)
            right = jnp.zeros((ROWS, 128), F32)
            for q in range(4):
                z = half * 4 + q
                a = v_ref[v, z, :, 0:128]
                a = pltpu.roll(a, q * 24, 1) if q else a
                b = pltpu.roll(v_ref[v, z, :, 128:256], q * 24 + 24, 1)
                left = jnp.where(lane == q, a, left)
                right = jnp.where(lane == q, b, right)
            left_ref[v, :, half * 128 : half * 128 + 128] = left
            right_ref[v, :, half * 128 : half * 128 + 128] = right


def pack_views(views):
    return pl.pallas_call(
        pack_views_kernel,
        out_shape=[jax.ShapeDtypeStruct((VIEWS, ROWS, COLS), F32)] * 2,
        in_specs=[VMEM],
        out_specs=[VMEM] * 2,
        name="pack_views",
        cost_estimate=pl.CostEstimate(flops=1_000_000, bytes_accessed=2_600_000, transcendentals=0),
    )(views)


def pack_rows_kernel(e_ref, l_ref, r_ref, first_ref, last_ref):
    for out_ref, start in ((first_ref, 0), (last_ref, ROWS - EDGE)):
        for z in range(Z):
            out_ref[z * EDGE : (z + 1) * EDGE, :] = e_ref[z, start : start + EDGE, :]
        out_ref[Z * EDGE :, 0:128] = l_ref[start : start + EDGE, :]
        out_ref[Z * EDGE :, 128:256] = r_ref[start : start + EDGE, :]


def pack_rows(estimate, left, right):
    return pl.pallas_call(
        pack_rows_kernel,
        out_shape=[jax.ShapeDtypeStruct(((Z + 1) * EDGE, COLS), F32)] * 2,
        in_specs=[VMEM] * 3,
        out_specs=[VMEM] * 2,
        name="pack_rows",
    )(estimate, left, right)


def warp_kernel(p_ref, v_ref, l_ref, r_ref, wi_ref, si_ref, wo_ref, so_ref,
                src, c_hi, c_lo, s_hi, s_lo):
    v = pl.program_id(0)
    j, i = p_ref[180], p_ref[181]
    lane = iota((ROWS, 128), 1)
    for z in range(Z):
        q, half = z % 4, z // 4
        a, b = v_ref[0, z, :, 0:128], v_ref[0, z, :, 128:256]
        left = l_ref[0, :, half * 128 : half * 128 + 128]
        right = r_ref[0, :, half * 128 : half * 128 + 128]
        left = pltpu.roll(left, (128 - q * 24) % 128, 1) if q else left
        right = pltpu.roll(right, (128 + 24 - q * 24) % 128, 1) if q != 1 else right
        edge = jnp.where(lane < 24, left, jnp.where(lane < 48, right, jnp.where(
            lane < 64, pltpu.roll(a, 48, 1), jnp.where(lane < 80, pltpu.roll(b, 80, 1), 0.0))))
        for t, part in enumerate((a, b, edge)):
            high, low = split(part)
            src[z * 128 : z * 128 + 64, t * 128 : t * 128 + 128] = high
            src[z * 128 + 64 : z * 128 + 128, t * 128 : t * 128 + 128] = low
    src[Z * 128 :, :] = jnp.zeros((128, 384), BF16)

    def offset(axis, b, c):
        return p_ref[((v * 2 + axis) * 3 + b) * 3 + c]

    def quarter(axis, b, c):
        return p_ref[72 + ((v * 3 + axis) * 3 + b) * 3 + c].astype(F32) * 0.25

    shape = (96, 256)
    row = iota(shape, 0)
    source = iota(shape, 1)
    upper_plane = source >= 128
    source = source & 63
    target = jnp.where(row < 48, row + 8, jnp.where(row < 56, row - 48, jnp.where(
        row < 64, row, jnp.where(row < 80, row - 80, row - 16))))

    def rows_matrix(c):
        def pick(values):
            return jnp.where(row < 64, values[1], jnp.where(row < 80, values[0], values[2]))

        good_c = (i > 0) if c == 0 else ((i < p_ref[183]) if c == 2 else (i >= 0))
        good = [((j > 0) & good_c).astype(F32), good_c.astype(F32), ((j < p_ref[182]) & good_c).astype(F32)]
        shift = pick([offset(1, b, c) for b in range(3)])
        f_y = pick([quarter(1, b, c) for b in range(3)])
        f_z0 = pick([(1.0 - quarter(2, b, c)) * good[b] for b in range(3)])
        f_z1 = pick([quarter(2, b, c) * good[b] for b in range(3)])
        tap = source - target - shift
        weight = jnp.where(tap == 0, 1.0 - f_y, jnp.where(tap == 1, f_y, 0.0))
        return (weight * jnp.where(upper_plane, f_z1, f_z0)).astype(BF16)

    center = rows_matrix(1)
    sides = jnp.concatenate([rows_matrix(0), rows_matrix(2)], axis=0)
    for z in range(Z):
        data = src[z * 128 : z * 128 + 256, :]
        c = jnp.dot(center, data, preferred_element_type=F32)
        s = jnp.dot(sides, data[:, 256:384], preferred_element_type=F32)
        for value, hi_ref, lo_ref, col, width in (
            (c, c_hi, c_lo, 0, 384), (s[0:96], s_hi, s_lo, 0, 128), (s[96:192], s_hi, s_lo, 128, 128)):
            high, low = split(value)
            for ref, part in ((hi_ref, high), (lo_ref, low)):
                ref[z * 64 : z * 64 + 64, col : col + width] = part[0:64]
                ref[512 + z * 16 : 528 + z * 16, col : col + width] = part[64:80]
                ref[640 + z * 16 : 656 + z * 16, col : col + width] = part[80:96]

    for b, start, count in ((1, 0, 512), (0, 512, 128), (2, 640, 128)):
        k = iota((384, COLS), 0)
        col = jnp.where(k < 256, k, jnp.where(k < 280, k - 280, jnp.where(k < 304, k - 24, 8192)))
        tap = col - iota((384, COLS), 1) - offset(0, b, 1)
        f_x = quarter(0, b, 1)
        x_map = jnp.where(tap == 0, 1.0 - f_x, jnp.where(tap == 1, f_x, 0.0)).astype(BF16)
        k = iota((256, 128), 0)
        is_right = k >= 128
        h = k & 127
        col = jnp.where(h < 24, h - 24, jnp.where(h < 48, h + 232, jnp.where(
            h < 64, h - 48, jnp.where(h < 80, h + 176, 8192))))
        out_lane = iota((256, 128), 1)
        right_lane = out_lane >= 8
        tap = col - strip_col(out_lane) - jnp.where(is_right, offset(0, b, 2), offset(0, b, 0))
        tap = jnp.where(is_right == right_lane, tap, -1)
        f_x = jnp.where(is_right, quarter(0, b, 2), quarter(0, b, 0))
        s_map = jnp.where(tap == 0, 1.0 - f_x, jnp.where(tap == 1, f_x, 0.0)).astype(BF16)
        rows = slice(start, start + count)
        w = jnp.dot(c_hi[rows], x_map, preferred_element_type=F32)
        w += jnp.dot(c_lo[rows], x_map, preferred_element_type=F32)
        s = jnp.dot(s_hi[rows], s_map, preferred_element_type=F32)
        s += jnp.dot(s_lo[rows], s_map, preferred_element_type=F32)
        for value, i_ref, o_ref in ((w, wi_ref, wo_ref), (s, si_ref, so_ref)):
            for z in range(Z):
                if b == 1:
                    i_ref[0, z] = value[z * 64 : z * 64 + 48]
                    o_ref[0, z, 0:16] = value[z * 64 + 48 : z * 64 + 64]
                else:
                    at = 16 if b == 0 else 32
                    o_ref[0, z, at : at + 16] = value[z * 16 : z * 16 + 16]


def warp(params, views, left, right):
    w = jax.ShapeDtypeStruct((VIEWS, Z, SET, COLS), F32)
    s = jax.ShapeDtypeStruct((VIEWS, Z, SET, 128), F32)
    w_spec = pl.BlockSpec((1, Z, SET, COLS), lambda v: (v, 0, 0, 0))
    s_spec = pl.BlockSpec((1, Z, SET, 128), lambda v: (v, 0, 0, 0))
    side = pl.BlockSpec((1, ROWS, COLS), lambda v: (v, 0, 0))
    return pl.pallas_call(
        warp_kernel,
        grid=(VIEWS,),
        out_shape=[w, s, w, s],
        in_specs=[SMEM, pl.BlockSpec((1, Z, ROWS, COLS), lambda v: (v, 0, 0, 0)), side, side],
        out_specs=[w_spec, s_spec, w_spec, s_spec],
        scratch_shapes=[
            pltpu.VMEM((9 * 128, 384), BF16),
            pltpu.VMEM((768, 384), BF16),
            pltpu.VMEM((768, 384), BF16),
            pltpu.VMEM((768, 256), BF16),
            pltpu.VMEM((768, 256), BF16),
        ],
        name="warp",
        cost_estimate=pl.CostEstimate(flops=6_000_000_000, bytes_accessed=8_000_000, transcendentals=0),
    )(params, views, left, right)


def main_kernel(inner, *refs):
    refs = list(refs)
    k_ref, e_ref, l_ref, r_ref = refs[:4]
    refs = refs[4:]
    if not inner:
        above, below = refs[:2]
        refs = refs[2:]
    w_ref, s_ref, ly, f_hi, f_lo, f_t, f_s, b_hi, b_lo, b_t, m_ref, n_ref = refs[:12]
    refs = refs[12:]
    if inner:
        out_refs, refs = refs[:1], refs[1:]
    else:
        partial_ref, out_refs, refs = refs[0], refs[1:4], refs[4:]
    d, g_hi, g_lo, g_t, cen, stp, q_hi, q_lo, q_t, x2 = refs
    count = estimate_rows(inner)
    lane = iota((count, 128), 1)
    lane_out = iota((VIEWS * SET, 128), 1)
    for z in range(Z):
        if inner:
            c0, c1 = e_ref[z, :, 0:128], e_ref[z, :, 128:256]
            lh, rh = l_ref[...], r_ref[...]
        else:
            edge = slice(z * EDGE, (z + 1) * EDGE)
            tail = slice(Z * EDGE, (Z + 1) * EDGE)

            def rows(cols, own):
                return jnp.concatenate(
                    [above[edge, cols], own[0:16], own[48:64], below[edge, cols]], axis=0)

            c0 = rows(slice(0, 128), e_ref[z, :, 0:128])
            c1 = rows(slice(128, 256), e_ref[z, :, 128:256])
            lh = jnp.concatenate(
                [above[tail, 0:128], l_ref[0:16], l_ref[48:64], below[tail, 0:128]], axis=0)
            rh = jnp.concatenate(
                [above[tail, 128:256], r_ref[0:16], r_ref[48:64], below[tail, 128:256]], axis=0)
        lh = pltpu.roll(lh, (128 - z * 16) % 128, 1) if z else lh
        rh = pltpu.roll(rh, (128 + 16 - z * 16) % 128, 1) if z != 1 else rh
        h = jnp.where(lane < 16, lh, jnp.where(lane < 32, rh, jnp.where(
            lane < 40, pltpu.roll(c0, 32, 1), jnp.where(lane < 48, pltpu.roll(c1, 48, 1), 0.0))))
        h = jnp.where(lane < 48, h, jnp.where(lane < 96, pltpu.roll(h, 48, 1), 0.0))
        for t, part in enumerate((c0, c1, h)):
            high, low = split(part)
            cols = slice(t * 128, t * 128 + 128)
            d[0:count, cols] = high
            d[count : 2 * count, cols] = low
            d[2 * count : 3 * count, cols] = high
        y = jnp.dot(ly[...], d[...], preferred_element_type=F32)
        high = y.astype(BF16)
        low = y - high.astype(F32)
        both = jnp.where(lane_out < 48, y[:, 256:384], low[:, 256:384]).astype(BF16)
        low = low.astype(BF16)
        for v in range(VIEWS):
            to, at = slice(z * SET, (z + 1) * SET), slice(v * SET, (v + 1) * SET)
            g_hi[v, to, :] = high[at, 0:256]
            g_lo[v, to, :] = low[at, 0:256]
            g_t[v, to, 0:128] = both[at]
            g_t[v, to, 128:256] = high[at, 256:384]

    def per_view(v, carry):
        def dot(a, b):
            return jnp.dot(a, b, preferred_element_type=F32)

        cen[...] = (dot(g_hi[v], f_hi[v]) + dot(g_lo[v], f_hi[v])) + (
            dot(g_hi[v], f_lo[v]) + dot(g_t[v], f_t[v]))
        stp[...] = dot(g_t[v], f_s[v])
        taps = [k_ref[2 * VIEWS * TAPS + v * TAPS + t] for t in range(TAPS)]
        for rb in range(3):
            for t in range(3):
                ref, cols = (cen, slice(t * 128, t * 128 + 128)) if t < 2 else (stp, slice(0, 128))
                at = [slice(z * SET + rb * 16, z * SET + rb * 16 + 16) for z in range(Z)]
                f = [ref[at[z], cols] for z in range(Z)]
                ratio = []
                for z in range(Z):
                    total = taps[7 - z] * f[0]
                    for y in range(1, Z):
                        total = total + taps[y - z + 7] * f[y]
                    total = jnp.where(total == 0.0, 1.0, total)
                    rows = slice(rb * 16, rb * 16 + 16)
                    top = w_ref[v, z, rows, cols] if t < 2 else s_ref[v, z, rows, cols]
                    ratio.append(top / total)
                for z in range(Z):
                    total = taps[z + 7] * ratio[0]
                    for y in range(1, Z):
                        total = total + taps[z - y + 7] * ratio[y]
                    if t < 2:
                        high, low = split(total)
                        q_hi[at[z], cols] = high
                        q_lo[at[z], cols] = low
                    else:
                        high = total.astype(BF16).astype(F32)
                        low = total - high
                        lanes = iota((16, 128), 1)
                        q_t[at[z], :] = jnp.where(lanes < 16, high, jnp.where(
                            lanes < 32, pltpu.roll(low, 16, 1), jnp.where(
                                lanes < 48, pltpu.roll(high, 32, 1), 0.0))).astype(BF16)
        x = (dot(q_hi[...], b_hi[v]) + dot(q_lo[...], b_hi[v])) + (
            dot(q_hi[...], b_lo[v]) + dot(q_t[...], b_t[v]))
        high, low = split(x)
        for z in range(Z):
            x2[z, 0, v] = high[z * SET : (z + 1) * SET]
            x2[z, 1, v] = low[z * SET : (z + 1) * SET]
        return carry

    lax.fori_loop(0, VIEWS, per_view, 0)
    for z in range(Z):
        high = x2[z, 0].reshape(VIEWS * SET, COLS)
        low = x2[z, 1].reshape(VIEWS * SET, COLS)
        out = jnp.dot(m_ref[...], high, preferred_element_type=F32)
        out += jnp.dot(m_ref[...], low, preferred_element_type=F32)
        out += jnp.dot(n_ref[...], high, preferred_element_type=F32)
        if inner:
            out_refs[0][z] = out
        else:
            out_refs[0][z] = out[0:64] + partial_ref[z]
            out_refs[1][z] = out[64:88]
            out_refs[2][z] = out[88:112]


def main(inner, *args):
    own = jax.ShapeDtypeStruct((Z, ROWS, COLS), F32)
    edge = jax.ShapeDtypeStruct((Z, EDGE, COLS), F32)
    rows = Z * SET
    return pl.pallas_call(
        functools.partial(main_kernel, inner),
        out_shape=[own] if inner else [own, edge, edge],
        in_specs=[SMEM] + [VMEM] * (len(args) - 1),
        out_specs=[VMEM] * (1 if inner else 3),
        scratch_shapes=[
            pltpu.VMEM((3 * estimate_rows(inner), 384), BF16),
            pltpu.VMEM((VIEWS, rows, 256), BF16),
            pltpu.VMEM((VIEWS, rows, 256), BF16),
            pltpu.VMEM((VIEWS, rows, 256), BF16),
            pltpu.VMEM((rows, 256), F32),
            pltpu.VMEM((rows, 128), F32),
            pltpu.VMEM((rows, 256), BF16),
            pltpu.VMEM((rows, 256), BF16),
            pltpu.VMEM((rows, 128), BF16),
            pltpu.VMEM((Z, 2, VIEWS, SET, COLS), BF16),
        ],
        name="inner_rows" if inner else "edge_rows",
        cost_estimate=pl.CostEstimate(flops=6_000_000_000, bytes_accessed=12_000_000, transcendentals=0),
    )(*args)


def final_kernel(e_ref, own_ref, up_ref, down_ref, out_ref):
    for z in range(Z):
        out_ref[z, 0:24] = e_ref[z, 0:24] * ((own_ref[z, 0:24] + up_ref[z]) * 0.25)
        out_ref[z, 24:40] = e_ref[z, 24:40] * (own_ref[z, 24:40] * 0.25)
        out_ref[z, 40:64] = e_ref[z, 40:64] * ((own_ref[z, 40:64] + down_ref[z]) * 0.25)


def final(*args):
    return pl.pallas_call(
        final_kernel,
        out_shape=jax.ShapeDtypeStruct((Z, ROWS, COLS), F32),
        in_specs=[VMEM] * 4,
        out_specs=VMEM,
        name="final",
    )(*args)


def shifted(first, last, axis):
    count = lax.axis_size(axis)
    up = [(i, i + 1) for i in range(count - 1)]
    down = [(i + 1, i) for i in range(count - 1)]
    return lax.ppermute(last, axis, up), lax.ppermute(first, axis, down)


def neighbours(table, j, i):
    padded = jnp.pad(table, ((0, 0), (0, 0), (1, 1), (1, 1)))
    zero = jnp.int32(0)
    return lax.dynamic_slice(padded, (zero, zero, j, i), table.shape[:2] + (3, 3)).reshape(-1)


def on_device(estimate, views, psf_x, psf_y, psf_z, block_offsets, sub_shifts):
    i, j = lax.axis_index("gx"), lax.axis_index("gy")
    psf = jnp.concatenate([psf_x, psf_y, psf_z], axis=0)
    kernels = (psf / jnp.sum(psf, axis=-1, keepdims=True)).reshape(-1)
    params = jnp.concatenate(
        [neighbours(block_offsets, j, i), neighbours(sub_shifts, j, i), j[None], i[None],
         jnp.array([lax.axis_size("gy") - 1, lax.axis_size("gx") - 1], jnp.int32)])
    e_left, e_right = shifted(*pack_estimate(estimate), "gx")
    mats = matrices(kernels)
    ly_i, ly_o, *x_mats, m_i, n_i, m_o, n_o = mats
    above, below = shifted(*pack_rows(estimate, e_left, e_right), "gy")
    v_left, v_right = shifted(*pack_views(views), "gx")
    w_i, s_i, w_o, s_o = warp(params, views, v_left, v_right)
    (inside,) = main(True, kernels, estimate, e_left, e_right, w_i, s_i, ly_i, *x_mats, m_i, n_i)
    own, up, down = main(
        False, kernels, estimate, e_left, e_right, above, below, w_o, s_o, ly_o, *x_mats,
        m_o, n_o, inside)
    from_above, from_below = shifted(up, down, "gy")
    return final(estimate, own, from_above, from_below)


def solution(mesh):
    in_specs = (P(None, "gy", "gx"), P(None, None, "gy", "gx"), P(), P(), P(), P(), P())
    out_specs = P(None, "gy", "gx")
    return jax.shard_map(
        on_device, mesh=mesh, in_specs=in_specs, out_specs=out_specs, check_vma=False
    )
```

```python
import functools

import jax
import jax.numpy as jnp
from jax import lax
from jax.experimental import pallas as pl
from jax.experimental.pallas import tpu as pltpu
from jax.sharding import PartitionSpec as P

F32 = jnp.float32
BF16 = jnp.bfloat16
VIEWS = 4
TAPS = 15
Z = 8
ROWS = 64
COLS = 256
SET = 48
EDGE = 24

SMEM = pl.BlockSpec(memory_space=pltpu.SMEM)
VMEM = pl.BlockSpec(memory_space=pltpu.VMEM)


EDGES = pl.BlockSpec((ROWS, COLS), lambda *g: (VIEWS, 0))


def limit(mib):
    return pltpu.CompilerParams(vmem_limit_bytes=mib << 20)


def iota(shape, dim):
    return lax.broadcasted_iota(jnp.int32, shape, dim)


def sample_row(inner, idx):
    if inner:
        return idx + 8
    return jnp.where(
        idx < 8, idx, jnp.where(idx < 16, idx + 48, jnp.where(idx < 32, idx - 32, idx + 32))
    )


def estimate_row(inner, idx):
    return idx if inner else jnp.where(idx < 40, idx - 24, idx + 8)


def output_row(inner, idx):
    return idx if inner else jnp.where(idx < 64, idx, jnp.where(idx < 88, idx - 88, idx - 24))


def estimate_rows(inner):
    return 64 if inner else 80


def output_rows(inner):
    return 64 if inner else 112


def strip_col(lane):
    return jnp.where(lane < 8, lane - 8, jnp.where(lane < 16, lane + 248, 4096))


def split(value):
    high = value.astype(BF16)
    return high, (value - high.astype(F32)).astype(BF16)


def band(k_ref, base, differ):
    total = jnp.zeros(differ.shape, F32)
    for tap in range(TAPS):
        total = jnp.where(differ == tap, k_ref[base + tap], total)
    return total


def matrices_kernel(k_ref, ly_i, ly_o, f_hi, f_lo, f_t, f_s, b_hi, b_lo, b_t, m_i, n_i, m_o, n_o):
    kx, ky = 0, VIEWS * TAPS
    for inner, ly in ((True, ly_i), (False, ly_o)):
        count = estimate_rows(inner)
        shape = (SET, 3 * count)
        lane = iota(shape, 1)
        seg = jnp.where(lane < count, 0, jnp.where(lane < 2 * count, 1, 2))
        differ = estimate_row(inner, lane - seg * count) - sample_row(inner, iota(shape, 0)) + 7
        for v in range(VIEWS):
            weight = band(k_ref, ky + v * TAPS, differ)
            high = weight.astype(BF16).astype(F32)
            ly[v * SET : (v + 1) * SET, :] = jnp.where(seg < 2, high, weight - high).astype(BF16)

    view = iota((1, VIEWS * SET), 1) // SET
    taps = []
    for tap in range(TAPS):
        value = jnp.full(view.shape, k_ref[ky + tap])
        for v in range(1, VIEWS):
            value = jnp.where(view == v, k_ref[ky + v * TAPS + tap], value)
        taps.append(value)
    for inner, m_ref, n_ref in ((True, m_i, n_i), (False, m_o, n_o)):
        shape = (output_rows(inner), VIEWS * SET)
        lane = iota(shape, 1)
        differ = output_row(inner, iota(shape, 0)) - sample_row(inner, lane - (lane // SET) * SET) + 7
        weight = jnp.zeros(shape, F32)
        for tap in range(TAPS):
            weight = jnp.where(differ == tap, taps[tap], weight)
        high, low = split(weight)
        m_ref[...] = high
        n_ref[...] = low

    def per_view(v, carry):
        base = kx + v * TAPS
        differ = iota((128, 128), 0) - iota((128, 128), 1) + 7
        corner = iota((16, 128), 0) - iota((16, 128), 1)
        for mirrored, hi_ref, lo_ref in ((False, f_hi, f_lo), (True, b_hi, b_lo)):
            def parts(d):
                return split(band(k_ref, base, 14 - d if mirrored else d))

            diagonal, lower, upper = parts(differ), parts(corner + 135), parts(corner - 9)
            for ref, a, b, c in zip((hi_ref, lo_ref), diagonal, lower, upper):
                ref[v, 0:128, 0:128] = a
                ref[v, 128:256, 128:256] = a
                ref[v, 128:144, 0:128] = b
                ref[v, 144:256, 0:128] = jnp.zeros((112, 128), BF16)
                ref[v, 112:128, 128:256] = c
                ref[v, 0:112, 128:256] = jnp.zeros((112, 128), BF16)
        for out_ref, width in ((f_t, COLS), (f_s, 128)):
            shape = (48, width)
            place = iota(shape, 0)
            source = jnp.where(
                place < 16,
                place - 16,
                jnp.where(place < 32, place + 240, jnp.where(place < 40, place - 32, place + 208)),
            )
            target = iota(shape, 1) if width == COLS else strip_col(iota(shape, 1))
            differ = source - target + 7
            if width == COLS:
                differ = jnp.where(place < 32, differ, -1)
            high, low = split(band(k_ref, base, differ))
            out_ref[v, 0:48] = high
            out_ref[v, 48:96] = high
            out_ref[v, 96:128] = jnp.zeros((32, width), BF16)
            out_ref[v, 128:176] = low
            out_ref[v, 176:256] = jnp.zeros((80, width), BF16)
        shape = (16, COLS)
        high, low = split(band(k_ref, base, iota(shape, 1) - strip_col(iota(shape, 0)) + 7))
        b_t[v, 0:16] = high
        b_t[v, 16:32] = high
        b_t[v, 32:48] = low
        b_t[v, 48:128] = jnp.zeros((80, COLS), BF16)
        return carry

    lax.fori_loop(0, VIEWS, per_view, 0)


def matrices(kernels):
    shapes = [
        (192, 192), (192, 240), (4, 256, 256), (4, 256, 256), (4, 256, 256), (4, 256, 128),
        (4, 256, 256), (4, 256, 256), (4, 128, 256), (64, 192), (64, 192), (112, 192), (112, 192),
    ]
    return pl.pallas_call(
        matrices_kernel,
        out_shape=[jax.ShapeDtypeStruct(s, BF16) for s in shapes],
        in_specs=[SMEM],
        out_specs=[VMEM] * len(shapes),
        name="matrices",
        compiler_params=limit(12),
        cost_estimate=pl.CostEstimate(flops=8_000_000, bytes_accessed=4_000_000, transcendentals=0),
    )(kernels)


def pack_edges_kernel(e_ref, v_ref, left_ref, right_ref):
    def fill(ref, count, width, base, lanes):
        lane = iota((ROWS, 128), 1) // width
        left = jnp.zeros((ROWS, 128), F32)
        right = jnp.zeros((ROWS, 128), F32)
        for q in range(count):
            a, b = ref(base + q, slice(0, 128)), ref(base + q, slice(128, 256))
            turn = (q * width + width) % 128
            a = pltpu.roll(a, q * width, 1) if q else a
            b = pltpu.roll(b, turn, 1) if turn else b
            left = jnp.where(lane == q, a, left)
            right = jnp.where(lane == q, b, right)
        left_ref[:, lanes] = left
        right_ref[:, lanes] = right

    @pl.when(pl.program_id(0) < VIEWS)
    def _():
        for half in range(2):
            fill(lambda z, cols: v_ref[0, z, :, cols], 4, 24, half * 4, slice(half * 128, half * 128 + 128))

    @pl.when(pl.program_id(0) == VIEWS)
    def _():
        fill(lambda z, cols: e_ref[z, :, cols], Z, 16, 0, slice(0, 128))
        for ref in (left_ref, right_ref):
            ref[:, 128:256] = jnp.zeros((ROWS, 128), F32)


def pack_edges(estimate, views):
    out = jax.ShapeDtypeStruct(((VIEWS + 1) * ROWS, COLS), F32)
    spec = pl.BlockSpec((ROWS, COLS), lambda g: (g, 0))
    return pl.pallas_call(
        pack_edges_kernel,
        grid=(VIEWS + 1,),
        out_shape=[out, out],
        in_specs=[
            pl.BlockSpec((Z, ROWS, COLS), lambda g: (0, 0, 0)),
            pl.BlockSpec((1, Z, ROWS, COLS), lambda g: (jnp.minimum(g, VIEWS - 1), 0, 0, 0)),
        ],
        out_specs=[spec, spec],
        name="pack_edges",
        compiler_params=limit(12),
        cost_estimate=pl.CostEstimate(flops=1_000_000, bytes_accessed=3_200_000, transcendentals=0),
    )(estimate, views)


def pack_rows_kernel(e_ref, l_ref, r_ref, first_ref, last_ref):
    for out_ref, start in ((first_ref, 0), (last_ref, ROWS - EDGE)):
        for z in range(Z):
            out_ref[z * EDGE : (z + 1) * EDGE, :] = e_ref[z, start : start + EDGE, :]
        out_ref[Z * EDGE :, 0:128] = l_ref[start : start + EDGE, 0:128]
        out_ref[Z * EDGE :, 128:256] = r_ref[start : start + EDGE, 0:128]


def pack_rows(estimate, left, right):
    return pl.pallas_call(
        pack_rows_kernel,
        out_shape=[jax.ShapeDtypeStruct(((Z + 1) * EDGE, COLS), F32)] * 2,
        in_specs=[VMEM, EDGES, EDGES],
        out_specs=[VMEM] * 2,
        grid=(1,),
        name="pack_rows",
        compiler_params=limit(12),
    )(estimate, left, right)


def planes_to_lanes(parts):
    lane = iota(parts[0].shape, 1) // 16
    total = parts[0]
    for z in range(1, Z):
        total = jnp.where(lane == z, pltpu.roll(parts[z], 16 * z, 1), total)
    return total


def warp_kernel(p_ref, v_ref, l_ref, r_ref, wi_ref, si_ref, wo_ref, so_ref,
                src, c_hi, c_lo, s_hi, s_lo):
    v = pl.program_id(0)
    j, i = p_ref[180], p_ref[181]
    lane = iota((ROWS, 128), 1)
    for z in range(Z):
        q, half = z % 4, z // 4
        a, b = v_ref[0, z, :, 0:128], v_ref[0, z, :, 128:256]
        left = l_ref[:, half * 128 : half * 128 + 128]
        right = r_ref[:, half * 128 : half * 128 + 128]
        left = pltpu.roll(left, (128 - q * 24) % 128, 1) if q else left
        right = pltpu.roll(right, (128 + 24 - q * 24) % 128, 1) if q != 1 else right
        edge = jnp.where(lane < 24, left, jnp.where(lane < 48, right, jnp.where(
            lane < 64, pltpu.roll(a, 48, 1), jnp.where(lane < 80, pltpu.roll(b, 80, 1), 0.0))))
        for t, part in enumerate((a, b, edge)):
            high, low = split(part)
            src[z * 128 : z * 128 + 64, t * 128 : t * 128 + 128] = high
            src[z * 128 + 64 : z * 128 + 128, t * 128 : t * 128 + 128] = low
    src[Z * 128 :, :] = jnp.zeros((128, 384), BF16)

    def offset(axis, b, c):
        return p_ref[((v * 2 + axis) * 3 + b) * 3 + c]

    def quarter(axis, b, c):
        return p_ref[72 + ((v * 3 + axis) * 3 + b) * 3 + c].astype(F32) * 0.25

    shape = (96, 256)
    row = iota(shape, 0)
    source = iota(shape, 1)
    upper_plane = source >= 128
    source = source & 63
    target = jnp.where(row < 48, row + 8, jnp.where(row < 56, row - 48, jnp.where(
        row < 64, row, jnp.where(row < 80, row - 80, row - 16))))

    def rows_matrix(c):
        def pick(values):
            return jnp.where(row < 64, values[1], jnp.where(row < 80, values[0], values[2]))

        good_c = (i > 0) if c == 0 else ((i < p_ref[183]) if c == 2 else (i >= 0))
        good = [((j > 0) & good_c).astype(F32), good_c.astype(F32), ((j < p_ref[182]) & good_c).astype(F32)]
        shift = pick([offset(1, b, c) for b in range(3)])
        f_y = pick([quarter(1, b, c) for b in range(3)])
        f_z0 = pick([(1.0 - quarter(2, b, c)) * good[b] for b in range(3)])
        f_z1 = pick([quarter(2, b, c) * good[b] for b in range(3)])
        tap = source - target - shift
        weight = jnp.where(tap == 0, 1.0 - f_y, jnp.where(tap == 1, f_y, 0.0))
        return (weight * jnp.where(upper_plane, f_z1, f_z0)).astype(BF16)

    center = rows_matrix(1)
    sides = jnp.concatenate([rows_matrix(0), rows_matrix(2)], axis=0)
    for z in range(Z):
        data = src[z * 128 : z * 128 + 256, :]
        c = jnp.dot(center, data, preferred_element_type=F32)
        s = jnp.dot(sides, data[:, 256:384], preferred_element_type=F32)
        for value, hi_ref, lo_ref, col, width in (
            (c, c_hi, c_lo, 0, 384), (s[0:96], s_hi, s_lo, 0, 128), (s[96:192], s_hi, s_lo, 128, 128)):
            high, low = split(value)
            for ref, part in ((hi_ref, high), (lo_ref, low)):
                ref[z * 64 : z * 64 + 64, col : col + width] = part[0:64]
                ref[512 + z * 16 : 528 + z * 16, col : col + width] = part[64:80]
                ref[640 + z * 16 : 656 + z * 16, col : col + width] = part[80:96]

    for b, start, count in ((1, 0, 512), (0, 512, 128), (2, 640, 128)):
        k = iota((384, COLS), 0)
        col = jnp.where(k < 256, k, jnp.where(k < 280, k - 280, jnp.where(k < 304, k - 24, 8192)))
        tap = col - iota((384, COLS), 1) - offset(0, b, 1)
        f_x = quarter(0, b, 1)
        x_map = jnp.where(tap == 0, 1.0 - f_x, jnp.where(tap == 1, f_x, 0.0)).astype(BF16)
        k = iota((256, 128), 0)
        is_right = k >= 128
        h = k & 127
        col = jnp.where(h < 24, h - 24, jnp.where(h < 48, h + 232, jnp.where(
            h < 64, h - 48, jnp.where(h < 80, h + 176, 8192))))
        out_lane = iota((256, 128), 1)
        right_lane = out_lane >= 8
        tap = col - strip_col(out_lane) - jnp.where(is_right, offset(0, b, 2), offset(0, b, 0))
        tap = jnp.where(is_right == right_lane, tap, -1)
        f_x = jnp.where(is_right, quarter(0, b, 2), quarter(0, b, 0))
        s_map = jnp.where(tap == 0, 1.0 - f_x, jnp.where(tap == 1, f_x, 0.0)).astype(BF16)
        rows = slice(start, start + count)
        w = jnp.dot(c_hi[rows], x_map, preferred_element_type=F32)
        w += jnp.dot(c_lo[rows], x_map, preferred_element_type=F32)
        s = jnp.dot(s_hi[rows], s_map, preferred_element_type=F32)
        s += jnp.dot(s_lo[rows], s_map, preferred_element_type=F32)
        at = 0 if b == 1 else (16 if b == 0 else 32)
        for z in range(Z):
            if b == 1:
                wi_ref[0, z] = w[z * 64 : z * 64 + 48]
                wo_ref[0, z, 0:16] = w[z * 64 + 48 : z * 64 + 64]
            else:
                wo_ref[0, z, at : at + 16] = w[z * 16 : z * 16 + 16]
        if b == 1:
            si_ref[0] = planes_to_lanes([s[z * 64 : z * 64 + 48] for z in range(Z)])
            so_ref[0, 0:16] = planes_to_lanes([s[z * 64 + 48 : z * 64 + 64] for z in range(Z)])
        else:
            so_ref[0, at : at + 16] = planes_to_lanes([s[z * 16 : z * 16 + 16] for z in range(Z)])


def warp(params, views, left, right):
    w = jax.ShapeDtypeStruct((VIEWS, Z, SET, COLS), F32)
    s = jax.ShapeDtypeStruct((VIEWS, SET, 128), F32)
    w_spec = pl.BlockSpec((1, Z, SET, COLS), lambda v: (v, 0, 0, 0))
    s_spec = pl.BlockSpec((1, SET, 128), lambda v: (v, 0, 0))
    side = pl.BlockSpec((ROWS, COLS), lambda v: (v, 0))
    return pl.pallas_call(
        warp_kernel,
        grid=(VIEWS,),
        out_shape=[w, s, w, s],
        in_specs=[SMEM, pl.BlockSpec((1, Z, ROWS, COLS), lambda v: (v, 0, 0, 0)), side, side],
        out_specs=[w_spec, s_spec, w_spec, s_spec],
        scratch_shapes=[
            pltpu.VMEM((9 * 128, 384), BF16),
            pltpu.VMEM((768, 384), BF16),
            pltpu.VMEM((768, 384), BF16),
            pltpu.VMEM((768, 256), BF16),
            pltpu.VMEM((768, 256), BF16),
        ],
        name="warp",
        compiler_params=limit(20),
        cost_estimate=pl.CostEstimate(flops=6_000_000_000, bytes_accessed=8_000_000, transcendentals=0),
    )(params, views, left, right)


def main_kernel(inner, *refs):
    refs = list(refs)
    k_ref, e_ref, l_ref, r_ref = refs[:4]
    refs = refs[4:]
    if not inner:
        above, below = refs[:2]
        refs = refs[2:]
    w_ref, s_ref, ly, f_hi, f_lo, f_t, f_s, b_hi, b_lo, b_t, m_ref, n_ref = refs[:12]
    refs = refs[12:]
    if inner:
        out_refs, refs = refs[:1], refs[1:]
    else:
        partial_ref, out_refs, refs = refs[0], refs[1:4], refs[4:]
    d, g_hi, g_lo, g_t, cen, q_hi, q_lo, q_t, x2 = refs
    count = estimate_rows(inner)
    lane = iota((count, 128), 1)
    lane_out = iota((VIEWS * SET, 128), 1)
    for z in range(Z):
        if inner:
            c0, c1 = e_ref[z, :, 0:128], e_ref[z, :, 128:256]
            lh, rh = l_ref[:, 0:128], r_ref[:, 0:128]
        else:
            edge = slice(z * EDGE, (z + 1) * EDGE)
            tail = slice(Z * EDGE, (Z + 1) * EDGE)

            def rows(cols, own):
                return jnp.concatenate(
                    [above[edge, cols], own[0:16], own[48:64], below[edge, cols]], axis=0)

            c0 = rows(slice(0, 128), e_ref[z, :, 0:128])
            c1 = rows(slice(128, 256), e_ref[z, :, 128:256])
            lh = jnp.concatenate(
                [above[tail, 0:128], l_ref[0:16, 0:128], l_ref[48:64, 0:128], below[tail, 0:128]], axis=0)
            rh = jnp.concatenate(
                [above[tail, 128:256], r_ref[0:16, 0:128], r_ref[48:64, 0:128], below[tail, 128:256]], axis=0)
        lh = pltpu.roll(lh, (128 - z * 16) % 128, 1) if z else lh
        rh = pltpu.roll(rh, (128 + 16 - z * 16) % 128, 1) if z != 1 else rh
        h = jnp.where(lane < 16, lh, jnp.where(lane < 32, rh, jnp.where(
            lane < 40, pltpu.roll(c0, 32, 1), jnp.where(lane < 48, pltpu.roll(c1, 48, 1), 0.0))))
        h = jnp.where(lane < 48, h, jnp.where(lane < 96, pltpu.roll(h, 48, 1), 0.0))
        for t, part in enumerate((c0, c1, h)):
            high, low = split(part)
            cols = slice(t * 128, t * 128 + 128)
            d[0:count, cols] = high
            d[count : 2 * count, cols] = low
            d[2 * count : 3 * count, cols] = high
        y = jnp.dot(ly[...], d[...], preferred_element_type=F32)
        high = y.astype(BF16)
        low = y - high.astype(F32)
        both = jnp.where(lane_out < 48, y[:, 256:384], low[:, 256:384]).astype(BF16)
        low = low.astype(BF16)
        for v in range(VIEWS):
            to, at = slice(z * SET, (z + 1) * SET), slice(v * SET, (v + 1) * SET)
            g_hi[v, to, :] = high[at, 0:256]
            g_lo[v, to, :] = low[at, 0:256]
            g_t[v, to, 0:128] = both[at]
            g_t[v, to, 128:256] = high[at, 256:384]

    def dot(a, b):
        return jnp.dot(a, b, preferred_element_type=F32)

    plane = iota((SET, 128), 1) // 16
    lanes = iota((SET, 128), 1)

    def turn(value, by):
        return pltpu.roll(value, by % 128, 1) if by % 128 else value

    for v in range(VIEWS):
        cen[v] = (dot(g_hi[v], f_hi[v]) + dot(g_lo[v], f_hi[v])) + (
            dot(g_hi[v], f_lo[v]) + dot(g_t[v], f_t[v]))
        strip = dot(g_t[v], f_s[v])
        taps = [k_ref[2 * VIEWS * TAPS + v * TAPS + t] for t in range(TAPS)]
        for rb in range(3):
            for t in range(2):
                cols = slice(t * 128, t * 128 + 128)
                at = [slice(z * SET + rb * 16, z * SET + rb * 16 + 16) for z in range(Z)]
                f = [cen[v, at[z], cols] for z in range(Z)]
                ratio = []
                for z in range(Z):
                    total = taps[7 - z] * f[0]
                    for y in range(1, Z):
                        total = total + taps[y - z + 7] * f[y]
                    total = jnp.where(total == 0.0, 1.0, total)
                    ratio.append(w_ref[v, z, rb * 16 : rb * 16 + 16, cols] / total)
                for z in range(Z):
                    total = taps[z + 7] * ratio[0]
                    for y in range(1, Z):
                        total = total + taps[z - y + 7] * ratio[y]
                    high, low = split(total)
                    q_hi[v, at[z], cols] = high
                    q_lo[v, at[z], cols] = low
        strip = planes_to_lanes([strip[z * SET : (z + 1) * SET] for z in range(Z)])
        total = taps[7] * strip
        for y in range(1, Z):
            total = total + jnp.where(plane < Z - y, taps[7 + y], taps[y - 1]) * turn(strip, -16 * y)
        ratio = s_ref[v] / jnp.where(total == 0.0, 1.0, total)
        total = taps[7] * ratio
        for y in range(1, Z):
            total = total + jnp.where(plane < Z - y, taps[7 - y], taps[15 - y]) * turn(ratio, -16 * y)
        high = total.astype(BF16).astype(F32)
        low = total - high
        for z in range(Z):
            q_t[v, z * SET : (z + 1) * SET, :] = jnp.where(lanes < 16, turn(high, -16 * z), jnp.where(
                lanes < 32, turn(low, 16 - 16 * z), jnp.where(
                    lanes < 48, turn(high, 32 - 16 * z), 0.0))).astype(BF16)
        x = (dot(q_hi[v], b_hi[v]) + dot(q_lo[v], b_hi[v])) + (
            dot(q_hi[v], b_lo[v]) + dot(q_t[v], b_t[v]))
        high, low = split(x)
        for z in range(Z):
            x2[z, 0, v] = high[z * SET : (z + 1) * SET]
            x2[z, 1, v] = low[z * SET : (z + 1) * SET]
    for z in range(Z):
        high = x2[z, 0].reshape(VIEWS * SET, COLS)
        low = x2[z, 1].reshape(VIEWS * SET, COLS)
        out = jnp.dot(m_ref[...], high, preferred_element_type=F32)
        out += jnp.dot(m_ref[...], low, preferred_element_type=F32)
        out += jnp.dot(n_ref[...], high, preferred_element_type=F32)
        if inner:
            out_refs[0][z] = out
        else:
            out_refs[0][z] = out[0:64] + partial_ref[z]
            out_refs[1][z] = out[64:88]
            out_refs[2][z] = out[88:112]


def main(inner, *args):
    own = jax.ShapeDtypeStruct((Z, ROWS, COLS), F32)
    edge = jax.ShapeDtypeStruct((Z, EDGE, COLS), F32)
    rows = Z * SET
    return pl.pallas_call(
        functools.partial(main_kernel, inner),
        out_shape=[own] if inner else [own, edge, edge],
        grid=(1,),
        in_specs=[SMEM, VMEM, EDGES, EDGES] + [VMEM] * (len(args) - 4),
        out_specs=[VMEM] * (1 if inner else 3),
        scratch_shapes=[
            pltpu.VMEM((3 * estimate_rows(inner), 384), BF16),
            pltpu.VMEM((VIEWS, rows, 256), BF16),
            pltpu.VMEM((VIEWS, rows, 256), BF16),
            pltpu.VMEM((VIEWS, rows, 256), BF16),
            pltpu.VMEM((VIEWS, rows, 256), F32),
            pltpu.VMEM((VIEWS, rows, 256), BF16),
            pltpu.VMEM((VIEWS, rows, 256), BF16),
            pltpu.VMEM((VIEWS, rows, 128), BF16),
            pltpu.VMEM((Z, 2, VIEWS, SET, COLS), BF16),
        ],
        name="inner_rows" if inner else "edge_rows",
        compiler_params=limit(28),
        cost_estimate=pl.CostEstimate(flops=6_000_000_000, bytes_accessed=12_000_000, transcendentals=0),
    )(*args)


def shifted(first, last, axis):
    count = lax.axis_size(axis)
    up = [(i, i + 1) for i in range(count - 1)]
    down = [(i + 1, i) for i in range(count - 1)]
    return lax.ppermute(last, axis, up), lax.ppermute(first, axis, down)


def neighbours(table, j, i):
    padded = jnp.pad(table, ((0, 0), (0, 0), (1, 1), (1, 1)))
    zero = jnp.int32(0)
    return lax.dynamic_slice(padded, (zero, zero, j, i), table.shape[:2] + (3, 3)).reshape(-1)


def on_device(estimate, views, psf_x, psf_y, psf_z, block_offsets, sub_shifts):
    i, j = lax.axis_index("gx"), lax.axis_index("gy")
    psf = jnp.concatenate([psf_x, psf_y, psf_z], axis=0)
    kernels = (psf / jnp.sum(psf, axis=-1, keepdims=True)).reshape(-1)
    params = jnp.concatenate(
        [neighbours(block_offsets, j, i), neighbours(sub_shifts, j, i), j[None], i[None],
         jnp.array([lax.axis_size("gy") - 1, lax.axis_size("gx") - 1], jnp.int32)])
    left, right = shifted(*pack_edges(estimate, views), "gx")
    mats = matrices(kernels)
    ly_i, ly_o, *x_mats, m_i, n_i, m_o, n_o = mats
    above, below = shifted(*pack_rows(estimate, left, right), "gy")
    w_i, s_i, w_o, s_o = warp(params, views, left, right)
    (inside,) = main(True, kernels, estimate, left, right, w_i, s_i, ly_i, *x_mats, m_i, n_i)
    own, up, down = main(
        False, kernels, estimate, left, right, above, below, w_o, s_o, ly_o, *x_mats,
        m_o, n_o, inside)
    from_above, from_below = shifted(up, down, "gy")
    rest = ROWS - EDGE
    total = own + jnp.pad(from_above, ((0, 0), (0, rest), (0, 0)))
    total = total + jnp.pad(from_below, ((0, 0), (rest, 0), (0, 0)))
    return estimate * (total * 0.25)


def solution(mesh):
    in_specs = (P(None, "gy", "gx"), P(None, None, "gy", "gx"), P(), P(), P(), P(), P())
    out_specs = P(None, "gy", "gx")
    return jax.shard_map(
        on_device, mesh=mesh, in_specs=in_specs, out_specs=out_specs, check_vma=False
    )
```

```python
import functools

import jax
import jax.numpy as jnp
from jax import lax
from jax.experimental import pallas as pl
from jax.experimental.pallas import tpu as pltpu
from jax.sharding import PartitionSpec as P

F32 = jnp.float32
BF16 = jnp.bfloat16
VIEWS = 4
TAPS = 15
Z = 8
ROWS = 64
COLS = 256
SET = 48
EDGE = 24

SMEM = pl.BlockSpec(memory_space=pltpu.SMEM)
VMEM = pl.BlockSpec(memory_space=pltpu.VMEM)


def limit(mib):
    return pltpu.CompilerParams(vmem_limit_bytes=mib << 20)


def iota(shape, dim):
    return lax.broadcasted_iota(jnp.int32, shape, dim)


def sample_row(inner, idx):
    if inner:
        return idx + 8
    return jnp.where(
        idx < 8, idx, jnp.where(idx < 16, idx + 48, jnp.where(idx < 32, idx - 32, idx + 32))
    )


def estimate_row(inner, idx):
    return idx if inner else jnp.where(idx < 40, idx - 24, idx + 8)


def output_row(inner, idx):
    return idx if inner else jnp.where(idx < 64, idx, jnp.where(idx < 88, idx - 88, idx - 24))


def estimate_rows(inner):
    return 64 if inner else 80


def output_rows(inner):
    return 64 if inner else 112


def strip_col(lane):
    return jnp.where(lane < 8, lane - 8, jnp.where(lane < 16, lane + 248, 4096))


def roll(value, by):
    return pltpu.roll(value, by % 128, 1) if by % 128 else value


def split(value):
    high = value.astype(BF16)
    return high, (value - high.astype(F32)).astype(BF16)


def band(k_ref, base, differ):
    total = jnp.zeros(differ.shape, F32)
    for tap in range(TAPS):
        total = jnp.where(differ == tap, k_ref[base + tap], total)
    return total


def matrices_kernel(k_ref, ly_i, ly_o, f_hi, f_lo, f_t, f_s, b_hi, b_lo, b_t, m_i, n_i, m_o, n_o):
    kx, ky = 0, VIEWS * TAPS
    for inner, ly in ((True, ly_i), (False, ly_o)):
        count = estimate_rows(inner)
        shape = (SET, 3 * count)
        lane = iota(shape, 1)
        seg = jnp.where(lane < count, 0, jnp.where(lane < 2 * count, 1, 2))
        differ = estimate_row(inner, lane - seg * count) - sample_row(inner, iota(shape, 0)) + 7
        for v in range(VIEWS):
            weight = band(k_ref, ky + v * TAPS, differ)
            high = weight.astype(BF16).astype(F32)
            ly[v * SET : (v + 1) * SET, :] = jnp.where(seg < 2, high, weight - high).astype(BF16)

    view = iota((1, VIEWS * SET), 1) // SET
    taps = []
    for tap in range(TAPS):
        value = jnp.full(view.shape, k_ref[ky + tap])
        for v in range(1, VIEWS):
            value = jnp.where(view == v, k_ref[ky + v * TAPS + tap], value)
        taps.append(value)
    for inner, m_ref, n_ref in ((True, m_i, n_i), (False, m_o, n_o)):
        shape = (output_rows(inner), VIEWS * SET)
        lane = iota(shape, 1)
        differ = output_row(inner, iota(shape, 0)) - sample_row(inner, lane - (lane // SET) * SET) + 7
        weight = jnp.zeros(shape, F32)
        for tap in range(TAPS):
            weight = jnp.where(differ == tap, taps[tap], weight)
        high, low = split(weight)
        m_ref[...] = high
        n_ref[...] = low

    def per_view(v, carry):
        base = kx + v * TAPS
        differ = iota((128, 128), 0) - iota((128, 128), 1) + 7
        corner = iota((16, 128), 0) - iota((16, 128), 1)
        for mirrored, hi_ref, lo_ref in ((False, f_hi, f_lo), (True, b_hi, b_lo)):
            def parts(d):
                return split(band(k_ref, base, 14 - d if mirrored else d))

            diagonal, lower, upper = parts(differ), parts(corner + 135), parts(corner - 9)
            for ref, a, b, c in zip((hi_ref, lo_ref), diagonal, lower, upper):
                ref[v, 0:128, 0:128] = a
                ref[v, 128:256, 128:256] = a
                ref[v, 128:144, 0:128] = b
                ref[v, 144:256, 0:128] = jnp.zeros((112, 128), BF16)
                ref[v, 112:128, 128:256] = c
                ref[v, 0:112, 128:256] = jnp.zeros((112, 128), BF16)
        for out_ref, width in ((f_t, COLS), (f_s, 128)):
            shape = (48, width)
            place = iota(shape, 0)
            source = jnp.where(
                place < 16,
                place - 16,
                jnp.where(place < 32, place + 240, jnp.where(place < 40, place - 32, place + 208)),
            )
            target = iota(shape, 1) if width == COLS else strip_col(iota(shape, 1))
            differ = source - target + 7
            if width == COLS:
                differ = jnp.where(place < 32, differ, -1)
            high, low = split(band(k_ref, base, differ))
            out_ref[v, 0:48] = high
            out_ref[v, 48:96] = high
            out_ref[v, 96:128] = jnp.zeros((32, width), BF16)
            out_ref[v, 128:176] = low
            out_ref[v, 176:256] = jnp.zeros((80, width), BF16)
        shape = (16, COLS)
        high, low = split(band(k_ref, base, iota(shape, 1) - strip_col(iota(shape, 0)) + 7))
        b_t[v, 0:16] = high
        b_t[v, 16:32] = high
        b_t[v, 32:48] = low
        b_t[v, 48:128] = jnp.zeros((80, COLS), BF16)
        return carry

    lax.fori_loop(0, VIEWS, per_view, 0)


def matrices(kernels):
    shapes = [
        (192, 192), (192, 240), (4, 256, 256), (4, 256, 256), (4, 256, 256), (4, 256, 128),
        (4, 256, 256), (4, 256, 256), (4, 128, 256), (64, 192), (64, 192), (112, 192), (112, 192),
    ]
    return pl.pallas_call(
        matrices_kernel,
        out_shape=[jax.ShapeDtypeStruct(s, BF16) for s in shapes],
        in_specs=[SMEM],
        out_specs=[VMEM] * len(shapes),
        name="matrices",
        compiler_params=limit(12),
        cost_estimate=pl.CostEstimate(flops=8_000_000, bytes_accessed=4_000_000, transcendentals=0),
    )(kernels)


def pack_edges_kernel(e_ref, v_ref, left_ref, right_ref):
    lane = iota((ROWS, 128), 1)
    for half in range(2):
        left = jnp.zeros((ROWS, 128), F32)
        right = jnp.zeros((ROWS, 128), F32)
        pieces = [(v_ref[0, half * 4 + q], q * 24, 24) for q in range(4)]
        if half == 0:
            pieces += [(e_ref[q], 96 + q * 16, 16) for q in range(2)]
        for plane, at, width in pieces:
            inside = (lane >= at) & (lane < at + width)
            left = jnp.where(inside, roll(plane[:, 0:128], at), left)
            right = jnp.where(inside, roll(plane[:, 128:256], at + width), right)
        left_ref[:, half * 128 : half * 128 + 128] = left
        right_ref[:, half * 128 : half * 128 + 128] = right


def pack_edges(estimate, views):
    out = jax.ShapeDtypeStruct((VIEWS * ROWS, COLS), F32)
    spec = pl.BlockSpec((ROWS, COLS), lambda v: (v, 0))
    return pl.pallas_call(
        pack_edges_kernel,
        grid=(VIEWS,),
        out_shape=[out, out],
        in_specs=[
            pl.BlockSpec((2, ROWS, COLS), lambda v: (v, 0, 0)),
            pl.BlockSpec((1, Z, ROWS, COLS), lambda v: (v, 0, 0, 0)),
        ],
        out_specs=[spec, spec],
        name="pack_edges",
        compiler_params=limit(12),
        cost_estimate=pl.CostEstimate(flops=1_000_000, bytes_accessed=3_200_000, transcendentals=0),
    )(estimate, views)


def pack_rows_kernel(e_ref, l_ref, r_ref, first_ref, last_ref, sides_ref):
    lane = iota((ROWS, 128), 1) // 32
    for ref, cols in ((l_ref, slice(0, 128)), (r_ref, slice(128, 256))):
        side = roll(ref[0:ROWS, 0:128], -96)
        for v in range(1, VIEWS):
            part = roll(ref[v * ROWS : (v + 1) * ROWS, 0:128], 32 * v - 96)
            side = jnp.where(lane == v, part, side)
        sides_ref[:, cols] = side
        first_ref[Z * EDGE :, cols] = side[0:EDGE]
        last_ref[Z * EDGE :, cols] = side[ROWS - EDGE :]
    for out_ref, start in ((first_ref, 0), (last_ref, ROWS - EDGE)):
        for z in range(Z):
            out_ref[z * EDGE : (z + 1) * EDGE, :] = e_ref[z, start : start + EDGE, :]


def pack_rows(estimate, left, right):
    rows = jax.ShapeDtypeStruct(((Z + 1) * EDGE, COLS), F32)
    return pl.pallas_call(
        pack_rows_kernel,
        out_shape=[rows, rows, jax.ShapeDtypeStruct((ROWS, COLS), F32)],
        in_specs=[VMEM] * 3,
        out_specs=[VMEM] * 3,
        name="pack_rows",
        compiler_params=limit(12),
    )(estimate, left, right)


def planes_to_lanes(parts):
    lane = iota(parts[0].shape, 1) // 16
    total = parts[0]
    for z in range(1, Z):
        total = jnp.where(lane == z, pltpu.roll(parts[z], 16 * z, 1), total)
    return total


def warp_kernel(p_ref, v_ref, l_ref, r_ref, wi_ref, si_ref, wo_ref, so_ref,
                src, c_hi, c_lo, s_hi, s_lo):
    v = pl.program_id(0)
    j, i = p_ref[180], p_ref[181]
    lane = iota((ROWS, 128), 1)
    for z in range(Z):
        q, half = z % 4, z // 4
        a, b = v_ref[0, z, :, 0:128], v_ref[0, z, :, 128:256]
        left = l_ref[:, half * 128 : half * 128 + 128]
        right = r_ref[:, half * 128 : half * 128 + 128]
        left = pltpu.roll(left, (128 - q * 24) % 128, 1) if q else left
        right = pltpu.roll(right, (128 + 24 - q * 24) % 128, 1) if q != 1 else right
        edge = jnp.where(lane < 24, left, jnp.where(lane < 48, right, jnp.where(
            lane < 64, pltpu.roll(a, 48, 1), jnp.where(lane < 80, pltpu.roll(b, 80, 1), 0.0))))
        for t, part in enumerate((a, b, edge)):
            high, low = split(part)
            src[z * 128 : z * 128 + 64, t * 128 : t * 128 + 128] = high
            src[z * 128 + 64 : z * 128 + 128, t * 128 : t * 128 + 128] = low
    src[Z * 128 :, :] = jnp.zeros((128, 384), BF16)

    def offset(axis, b, c):
        return p_ref[((v * 2 + axis) * 3 + b) * 3 + c]

    def quarter(axis, b, c):
        return p_ref[72 + ((v * 3 + axis) * 3 + b) * 3 + c].astype(F32) * 0.25

    shape = (96, 256)
    row = iota(shape, 0)
    source = iota(shape, 1)
    upper_plane = source >= 128
    source = source & 63
    target = jnp.where(row < 48, row + 8, jnp.where(row < 56, row - 48, jnp.where(
        row < 64, row, jnp.where(row < 80, row - 80, row - 16))))

    def rows_matrix(c):
        def pick(values):
            return jnp.where(row < 64, values[1], jnp.where(row < 80, values[0], values[2]))

        good_c = (i > 0) if c == 0 else ((i < p_ref[183]) if c == 2 else (i >= 0))
        good = [((j > 0) & good_c).astype(F32), good_c.astype(F32), ((j < p_ref[182]) & good_c).astype(F32)]
        shift = pick([offset(1, b, c) for b in range(3)])
        f_y = pick([quarter(1, b, c) for b in range(3)])
        f_z0 = pick([(1.0 - quarter(2, b, c)) * good[b] for b in range(3)])
        f_z1 = pick([quarter(2, b, c) * good[b] for b in range(3)])
        tap = source - target - shift
        weight = jnp.where(tap == 0, 1.0 - f_y, jnp.where(tap == 1, f_y, 0.0))
        return (weight * jnp.where(upper_plane, f_z1, f_z0)).astype(BF16)

    center = rows_matrix(1)
    sides = jnp.concatenate([rows_matrix(0), rows_matrix(2)], axis=0)
    for z in range(Z):
        data = src[z * 128 : z * 128 + 256, :]
        c = jnp.dot(center, data, preferred_element_type=F32)
        s = jnp.dot(sides, data[:, 256:384], preferred_element_type=F32)
        for value, hi_ref, lo_ref, col, width in (
            (c, c_hi, c_lo, 0, 384), (s[0:96], s_hi, s_lo, 0, 128), (s[96:192], s_hi, s_lo, 128, 128)):
            high, low = split(value)
            for ref, part in ((hi_ref, high), (lo_ref, low)):
                ref[z * 64 : z * 64 + 64, col : col + width] = part[0:64]
                ref[512 + z * 16 : 528 + z * 16, col : col + width] = part[64:80]
                ref[640 + z * 16 : 656 + z * 16, col : col + width] = part[80:96]

    for b, start, count in ((1, 0, 512), (0, 512, 128), (2, 640, 128)):
        k = iota((384, COLS), 0)
        col = jnp.where(k < 256, k, jnp.where(k < 280, k - 280, jnp.where(k < 304, k - 24, 8192)))
        tap = col - iota((384, COLS), 1) - offset(0, b, 1)
        f_x = quarter(0, b, 1)
        x_map = jnp.where(tap == 0, 1.0 - f_x, jnp.where(tap == 1, f_x, 0.0)).astype(BF16)
        k = iota((256, 128), 0)
        is_right = k >= 128
        h = k & 127
        col = jnp.where(h < 24, h - 24, jnp.where(h < 48, h + 232, jnp.where(
            h < 64, h - 48, jnp.where(h < 80, h + 176, 8192))))
        out_lane = iota((256, 128), 1)
        right_lane = out_lane >= 8
        tap = col - strip_col(out_lane) - jnp.where(is_right, offset(0, b, 2), offset(0, b, 0))
        tap = jnp.where(is_right == right_lane, tap, -1)
        f_x = jnp.where(is_right, quarter(0, b, 2), quarter(0, b, 0))
        s_map = jnp.where(tap == 0, 1.0 - f_x, jnp.where(tap == 1, f_x, 0.0)).astype(BF16)
        rows = slice(start, start + count)
        w = jnp.dot(c_hi[rows], x_map, preferred_element_type=F32)
        w += jnp.dot(c_lo[rows], x_map, preferred_element_type=F32)
        s = jnp.dot(s_hi[rows], s_map, preferred_element_type=F32)
        s += jnp.dot(s_lo[rows], s_map, preferred_element_type=F32)
        at = 0 if b == 1 else (16 if b == 0 else 32)
        for z in range(Z):
            if b == 1:
                wi_ref[0, z] = w[z * 64 : z * 64 + 48]
                wo_ref[0, z, 0:16] = w[z * 64 + 48 : z * 64 + 64]
            else:
                wo_ref[0, z, at : at + 16] = w[z * 16 : z * 16 + 16]
        if b == 1:
            si_ref[0] = planes_to_lanes([s[z * 64 : z * 64 + 48] for z in range(Z)])
            so_ref[0, 0:16] = planes_to_lanes([s[z * 64 + 48 : z * 64 + 64] for z in range(Z)])
        else:
            so_ref[0, at : at + 16] = planes_to_lanes([s[z * 16 : z * 16 + 16] for z in range(Z)])


def warp(params, views, left, right):
    w = jax.ShapeDtypeStruct((VIEWS, Z, SET, COLS), F32)
    s = jax.ShapeDtypeStruct((VIEWS, SET, 128), F32)
    w_spec = pl.BlockSpec((1, Z, SET, COLS), lambda v: (v, 0, 0, 0))
    s_spec = pl.BlockSpec((1, SET, 128), lambda v: (v, 0, 0))
    side = pl.BlockSpec((ROWS, COLS), lambda v: (v, 0))
    return pl.pallas_call(
        warp_kernel,
        grid=(VIEWS,),
        out_shape=[w, s, w, s],
        in_specs=[SMEM, pl.BlockSpec((1, Z, ROWS, COLS), lambda v: (v, 0, 0, 0)), side, side],
        out_specs=[w_spec, s_spec, w_spec, s_spec],
        scratch_shapes=[
            pltpu.VMEM((9 * 128, 384), BF16),
            pltpu.VMEM((768, 384), BF16),
            pltpu.VMEM((768, 384), BF16),
            pltpu.VMEM((768, 256), BF16),
            pltpu.VMEM((768, 256), BF16),
        ],
        name="warp",
        compiler_params=limit(20),
        cost_estimate=pl.CostEstimate(flops=6_000_000_000, bytes_accessed=8_000_000, transcendentals=0),
    )(params, views, left, right)


def main_kernel(inner, *refs):
    refs = list(refs)
    k_ref, e_ref, sides_ref = refs[:3]
    refs = refs[3:]
    if not inner:
        above, below = refs[:2]
        refs = refs[2:]
    w_ref, s_ref, ly, f_hi, f_lo, f_t, f_s, b_hi, b_lo, b_t, m_ref, n_ref = refs[:12]
    refs = refs[12:]
    if inner:
        out_refs, refs = refs[:1], refs[1:]
    else:
        out_refs, refs = refs[:3], refs[3:]
    d, g_hi, g_lo, g_t, cen, q_hi, q_lo, q_t, x2 = refs
    count = estimate_rows(inner)
    lane = iota((count, 128), 1)
    lane_out = iota((VIEWS * SET, 128), 1)
    for z in range(Z):
        if inner:
            c0, c1 = e_ref[z, :, 0:128], e_ref[z, :, 128:256]
            lh, rh = sides_ref[:, 0:128], sides_ref[:, 128:256]
        else:
            edge = slice(z * EDGE, (z + 1) * EDGE)
            tail = slice(Z * EDGE, (Z + 1) * EDGE)

            def rows(cols, own):
                return jnp.concatenate(
                    [above[edge, cols], own[0:16], own[48:64], below[edge, cols]], axis=0)

            c0 = rows(slice(0, 128), e_ref[z, :, 0:128])
            c1 = rows(slice(128, 256), e_ref[z, :, 128:256])
            lh = jnp.concatenate(
                [above[tail, 0:128], sides_ref[0:16, 0:128], sides_ref[48:64, 0:128], below[tail, 0:128]], axis=0)
            rh = jnp.concatenate(
                [above[tail, 128:256], sides_ref[0:16, 128:256], sides_ref[48:64, 128:256], below[tail, 128:256]], axis=0)
        lh = pltpu.roll(lh, (128 - z * 16) % 128, 1) if z else lh
        rh = pltpu.roll(rh, (128 + 16 - z * 16) % 128, 1) if z != 1 else rh
        h = jnp.where(lane < 16, lh, jnp.where(lane < 32, rh, jnp.where(
            lane < 40, pltpu.roll(c0, 32, 1), jnp.where(lane < 48, pltpu.roll(c1, 48, 1), 0.0))))
        h = jnp.where(lane < 48, h, jnp.where(lane < 96, pltpu.roll(h, 48, 1), 0.0))
        for t, part in enumerate((c0, c1, h)):
            high, low = split(part)
            cols = slice(t * 128, t * 128 + 128)
            d[0:count, cols] = high
            d[count : 2 * count, cols] = low
            d[2 * count : 3 * count, cols] = high
        y = jnp.dot(ly[...], d[...], preferred_element_type=F32)
        high = y.astype(BF16)
        low = y - high.astype(F32)
        both = jnp.where(lane_out < 48, y[:, 256:384], low[:, 256:384]).astype(BF16)
        low = low.astype(BF16)
        for v in range(VIEWS):
            to, at = slice(z * SET, (z + 1) * SET), slice(v * SET, (v + 1) * SET)
            g_hi[v, to, :] = high[at, 0:256]
            g_lo[v, to, :] = low[at, 0:256]
            g_t[v, to, 0:128] = both[at]
            g_t[v, to, 128:256] = high[at, 256:384]

    def dot(a, b):
        return jnp.dot(a, b, preferred_element_type=F32)

    plane = iota((SET, 128), 1) // 16
    lanes = iota((SET, 128), 1)

    def turn(value, by):
        return pltpu.roll(value, by % 128, 1) if by % 128 else value

    for v in range(VIEWS):
        cen[v] = (dot(g_hi[v], f_hi[v]) + dot(g_lo[v], f_hi[v])) + (
            dot(g_hi[v], f_lo[v]) + dot(g_t[v], f_t[v]))
        strip = dot(g_t[v], f_s[v])
        taps = [k_ref[2 * VIEWS * TAPS + v * TAPS + t] for t in range(TAPS)]
        for rb in range(3):
            for t in range(2):
                cols = slice(t * 128, t * 128 + 128)
                at = [slice(z * SET + rb * 16, z * SET + rb * 16 + 16) for z in range(Z)]
                f = [cen[v, at[z], cols] for z in range(Z)]
                ratio = []
                for z in range(Z):
                    total = taps[7 - z] * f[0]
                    for y in range(1, Z):
                        total = total + taps[y - z + 7] * f[y]
                    total = jnp.where(total == 0.0, 1.0, total)
                    ratio.append(w_ref[v, z, rb * 16 : rb * 16 + 16, cols] / total)
                for z in range(Z):
                    total = taps[z + 7] * ratio[0]
                    for y in range(1, Z):
                        total = total + taps[z - y + 7] * ratio[y]
                    high, low = split(total)
                    q_hi[v, at[z], cols] = high
                    q_lo[v, at[z], cols] = low
        strip = planes_to_lanes([strip[z * SET : (z + 1) * SET] for z in range(Z)])
        total = taps[7] * strip
        for y in range(1, Z):
            total = total + jnp.where(plane < Z - y, taps[7 + y], taps[y - 1]) * turn(strip, -16 * y)
        ratio = s_ref[v] / jnp.where(total == 0.0, 1.0, total)
        total = taps[7] * ratio
        for y in range(1, Z):
            total = total + jnp.where(plane < Z - y, taps[7 - y], taps[15 - y]) * turn(ratio, -16 * y)
        high = total.astype(BF16).astype(F32)
        low = total - high
        for z in range(Z):
            q_t[v, z * SET : (z + 1) * SET, :] = jnp.where(lanes < 16, turn(high, -16 * z), jnp.where(
                lanes < 32, turn(low, 16 - 16 * z), jnp.where(
                    lanes < 48, turn(high, 32 - 16 * z), 0.0))).astype(BF16)
        x = (dot(q_hi[v], b_hi[v]) + dot(q_lo[v], b_hi[v])) + (
            dot(q_hi[v], b_lo[v]) + dot(q_t[v], b_t[v]))
        high, low = split(x)
        for z in range(Z):
            x2[z, 0, v] = high[z * SET : (z + 1) * SET]
            x2[z, 1, v] = low[z * SET : (z + 1) * SET]
    for z in range(Z):
        high = x2[z, 0].reshape(VIEWS * SET, COLS)
        low = x2[z, 1].reshape(VIEWS * SET, COLS)
        out = jnp.dot(m_ref[...], high, preferred_element_type=F32)
        out += jnp.dot(m_ref[...], low, preferred_element_type=F32)
        out += jnp.dot(n_ref[...], high, preferred_element_type=F32)
        if inner:
            out_refs[0][z] = out
        else:
            out_refs[0][z] = out[0:64]
            out_refs[1][z] = out[64:88]
            out_refs[2][z] = out[88:112]


def main(inner, *args):
    own = jax.ShapeDtypeStruct((Z, ROWS, COLS), F32)
    edge = jax.ShapeDtypeStruct((Z, EDGE, COLS), F32)
    rows = Z * SET
    return pl.pallas_call(
        functools.partial(main_kernel, inner),
        out_shape=[own] if inner else [own, edge, edge],
        grid=(1,),
        in_specs=[SMEM] + [VMEM] * (len(args) - 1),
        out_specs=[VMEM] * (1 if inner else 3),
        scratch_shapes=[
            pltpu.VMEM((3 * estimate_rows(inner), 384), BF16),
            pltpu.VMEM((VIEWS, rows, 256), BF16),
            pltpu.VMEM((VIEWS, rows, 256), BF16),
            pltpu.VMEM((VIEWS, rows, 256), BF16),
            pltpu.VMEM((VIEWS, rows, 256), F32),
            pltpu.VMEM((VIEWS, rows, 256), BF16),
            pltpu.VMEM((VIEWS, rows, 256), BF16),
            pltpu.VMEM((VIEWS, rows, 128), BF16),
            pltpu.VMEM((Z, 2, VIEWS, SET, COLS), BF16),
        ],
        name="inner_rows" if inner else "edge_rows",
        compiler_params=limit(28),
        cost_estimate=pl.CostEstimate(flops=6_000_000_000, bytes_accessed=12_000_000, transcendentals=0),
    )(*args)


def shifted(first, last, axis):
    count = lax.axis_size(axis)
    up = [(i, i + 1) for i in range(count - 1)]
    down = [(i + 1, i) for i in range(count - 1)]
    return lax.ppermute(last, axis, up), lax.ppermute(first, axis, down)


def neighbours(table, j, i):
    padded = jnp.pad(table, ((0, 0), (0, 0), (1, 1), (1, 1)))
    zero = jnp.int32(0)
    return lax.dynamic_slice(padded, (zero, zero, j, i), table.shape[:2] + (3, 3)).reshape(-1)


def on_device(estimate, views, psf_x, psf_y, psf_z, block_offsets, sub_shifts):
    i, j = lax.axis_index("gx"), lax.axis_index("gy")
    psf = jnp.concatenate([psf_x, psf_y, psf_z], axis=0)
    kernels = (psf / jnp.sum(psf, axis=-1, keepdims=True)).reshape(-1)
    params = jnp.concatenate(
        [neighbours(block_offsets, j, i), neighbours(sub_shifts, j, i), j[None], i[None],
         jnp.array([lax.axis_size("gy") - 1, lax.axis_size("gx") - 1], jnp.int32)])
    left, right = shifted(*pack_edges(estimate, views), "gx")
    mats = matrices(kernels)
    ly_i, ly_o, *x_mats, m_i, n_i, m_o, n_o = mats
    first, last, sides = pack_rows(estimate, left, right)
    above, below = shifted(first, last, "gy")
    w_i, s_i, w_o, s_o = warp(params, views, left, right)
    own, up, down = main(
        False, kernels, estimate, sides, above, below, w_o, s_o, ly_o, *x_mats, m_o, n_o)
    w_i, own, up, down = lax.optimization_barrier((w_i, own, up, down))
    (inside,) = main(True, kernels, estimate, sides, w_i, s_i, ly_i, *x_mats, m_i, n_i)
    from_above, from_below = shifted(up, down, "gy")
    rest = ROWS - EDGE
    total = own + inside + jnp.pad(from_above, ((0, 0), (0, rest), (0, 0)))
    total = total + jnp.pad(from_below, ((0, 0), (rest, 0), (0, 0)))
    return estimate * (total * 0.25)


def solution(mesh):
    in_specs = (P(None, "gy", "gx"), P(None, None, "gy", "gx"), P(), P(), P(), P(), P())
    out_specs = P(None, "gy", "gx")
    return jax.shard_map(
        on_device, mesh=mesh, in_specs=in_specs, out_specs=out_specs, check_vma=False
    )
```

```python
import functools

import jax
import jax.numpy as jnp
from jax import lax
from jax.experimental import pallas as pl
from jax.experimental.pallas import tpu as pltpu
from jax.sharding import PartitionSpec as P


F32 = jnp.float32
BF16 = jnp.bfloat16
VIEWS = 4
TAPS = 15
Z = 8
ROWS = 64
COLS = 256
SET = 32
NEAR = 48
EDGE = 24

SMEM = pl.BlockSpec(memory_space=pltpu.SMEM)
VMEM = pl.BlockSpec(memory_space=pltpu.VMEM)


def limit(mib):
    return pltpu.CompilerParams(vmem_limit_bytes=mib << 20)


def iota(shape, dim):
    return lax.broadcasted_iota(jnp.int32, shape, dim)


def strip_col(lane):
    return jnp.where(lane < 8, lane - 8, jnp.where(lane < 16, lane + 248, 4096))


def roll(value, by):
    return pltpu.roll(value, by % 128, 1) if by % 128 else value


def split(value):
    high = value.astype(BF16)
    return high, (value - high.astype(F32)).astype(BF16)


def band(k_ref, base, differ):
    total = jnp.zeros(differ.shape, F32)
    for tap in range(TAPS):
        total = jnp.where(differ == tap, k_ref[base + tap], total)
    return total


def matrices_kernel(k_ref, ly, f_hi, f_lo, f_t, f_s, b_hi, b_lo, b_t, m_ref, n_ref):
    kx, ky = 0, VIEWS * TAPS
    shape = (SET, 3 * NEAR)
    lane = iota(shape, 1)
    seg = jnp.where(lane < NEAR, 0, jnp.where(lane < 2 * NEAR, 1, 2))
    differ = lane - seg * NEAR - iota(shape, 0) - 1
    for v in range(VIEWS):
        weight = band(k_ref, ky + v * TAPS, differ)
        high = weight.astype(BF16).astype(F32)
        ly[v * SET : (v + 1) * SET, :] = jnp.where(seg < 2, high, weight - high).astype(BF16)

    view = iota((1, VIEWS * SET), 1) // SET
    taps = []
    for tap in range(TAPS):
        value = jnp.full(view.shape, k_ref[ky + tap])
        for v in range(1, VIEWS):
            value = jnp.where(view == v, k_ref[ky + v * TAPS + tap], value)
        taps.append(value)
    shape = (NEAR, VIEWS * SET)
    differ = iota(shape, 0) - (iota(shape, 1) & (SET - 1)) - 1
    weight = jnp.zeros(shape, F32)
    for tap in range(TAPS):
        weight = jnp.where(differ == tap, taps[tap], weight)
    high, low = split(weight)
    m_ref[...] = high
    n_ref[...] = low

    def per_view(v, carry):
        base = kx + v * TAPS
        differ = iota((128, 128), 0) - iota((128, 128), 1) + 7
        corner = iota((16, 128), 0) - iota((16, 128), 1)
        for mirrored, hi_ref, lo_ref in ((False, f_hi, f_lo), (True, b_hi, b_lo)):
            def parts(d):
                return split(band(k_ref, base, 14 - d if mirrored else d))

            diagonal, lower, upper = parts(differ), parts(corner + 135), parts(corner - 9)
            for ref, a, b, c in zip((hi_ref, lo_ref), diagonal, lower, upper):
                ref[v, 0:128, 0:128] = a
                ref[v, 128:256, 128:256] = a
                ref[v, 128:144, 0:128] = b
                ref[v, 144:256, 0:128] = jnp.zeros((112, 128), BF16)
                ref[v, 112:128, 128:256] = c
                ref[v, 0:112, 128:256] = jnp.zeros((112, 128), BF16)
        for out_ref, width in ((f_t, COLS), (f_s, 128)):
            shape = (48, width)
            place = iota(shape, 0)
            source = jnp.where(
                place < 16,
                place - 16,
                jnp.where(place < 32, place + 240, jnp.where(place < 40, place - 32, place + 208)),
            )
            target = iota(shape, 1) if width == COLS else strip_col(iota(shape, 1))
            differ = source - target + 7
            if width == COLS:
                differ = jnp.where(place < 32, differ, -1)
            high, low = split(band(k_ref, base, differ))
            out_ref[v, 0:48] = high
            out_ref[v, 48:96] = high
            out_ref[v, 96:128] = jnp.zeros((32, width), BF16)
            out_ref[v, 128:176] = low
            out_ref[v, 176:256] = jnp.zeros((80, width), BF16)
        shape = (16, COLS)
        high, low = split(band(k_ref, base, iota(shape, 1) - strip_col(iota(shape, 0)) + 7))
        b_t[v, 0:16] = high
        b_t[v, 16:32] = high
        b_t[v, 32:48] = low
        b_t[v, 48:128] = jnp.zeros((80, COLS), BF16)
        return carry

    lax.fori_loop(0, VIEWS, per_view, 0)


def matrices(kernels):
    shapes = [
        (128, 144), (4, 256, 256), (4, 256, 256), (4, 256, 256), (4, 256, 128),
        (4, 256, 256), (4, 256, 256), (4, 128, 256), (48, 128), (48, 128),
    ]
    return pl.pallas_call(
        matrices_kernel,
        out_shape=[jax.ShapeDtypeStruct(s, BF16) for s in shapes],
        in_specs=[SMEM],
        out_specs=[VMEM] * len(shapes),
        name="matrices",
        compiler_params=limit(12),
        cost_estimate=pl.CostEstimate(flops=8_000_000, bytes_accessed=4_000_000, transcendentals=0),
    )(kernels)


def pack_edges_kernel(e_ref, v_ref, left_ref, right_ref):
    lane = iota((ROWS, 128), 1)
    for half in range(2):
        left = jnp.zeros((ROWS, 128), F32)
        right = jnp.zeros((ROWS, 128), F32)
        pieces = [(v_ref[0, half * 4 + q], q * 24, 24) for q in range(4)]
        if half == 0:
            pieces += [(e_ref[q], 96 + q * 16, 16) for q in range(2)]
        for plane, at, width in pieces:
            inside = (lane >= at) & (lane < at + width)
            left = jnp.where(inside, roll(plane[:, 0:128], at), left)
            right = jnp.where(inside, roll(plane[:, 128:256], at + width), right)
        left_ref[:, half * 128 : half * 128 + 128] = left
        right_ref[:, half * 128 : half * 128 + 128] = right


def pack_edges(estimate, views):
    out = jax.ShapeDtypeStruct((VIEWS * ROWS, COLS), F32)
    spec = pl.BlockSpec((ROWS, COLS), lambda v: (v, 0))
    return pl.pallas_call(
        pack_edges_kernel,
        grid=(VIEWS,),
        out_shape=[out, out],
        in_specs=[
            pl.BlockSpec((2, ROWS, COLS), lambda v: (v, 0, 0)),
            pl.BlockSpec((1, Z, ROWS, COLS), lambda v: (v, 0, 0, 0)),
        ],
        out_specs=[spec, spec],
        name="pack_edges",
        compiler_params=limit(12),
        cost_estimate=pl.CostEstimate(flops=1_000_000, bytes_accessed=3_200_000, transcendentals=0),
    )(estimate, views)


def pack_rows_kernel(e_ref, l_ref, r_ref, first_ref, last_ref, sides_ref):
    lane = iota((ROWS, 128), 1) // 32
    for ref, cols in ((l_ref, slice(0, 128)), (r_ref, slice(128, 256))):
        side = roll(ref[0:ROWS, 0:128], -96)
        for v in range(1, VIEWS):
            part = roll(ref[v * ROWS : (v + 1) * ROWS, 0:128], 32 * v - 96)
            side = jnp.where(lane == v, part, side)
        sides_ref[:, cols] = side
        first_ref[Z * EDGE :, cols] = side[0:EDGE]
        last_ref[Z * EDGE :, cols] = side[ROWS - EDGE :]
    for out_ref, start in ((first_ref, 0), (last_ref, ROWS - EDGE)):
        for z in range(Z):
            out_ref[z * EDGE : (z + 1) * EDGE, :] = e_ref[z, start : start + EDGE, :]


def pack_rows(estimate, left, right):
    rows = jax.ShapeDtypeStruct(((Z + 1) * EDGE, COLS), F32)
    return pl.pallas_call(
        pack_rows_kernel,
        out_shape=[rows, rows, jax.ShapeDtypeStruct((ROWS, COLS), F32)],
        in_specs=[VMEM] * 3,
        out_specs=[VMEM] * 3,
        name="pack_rows",
        compiler_params=limit(12),
    )(estimate, left, right)


def planes_to_lanes(parts):
    lane = iota(parts[0].shape, 1) // 16
    total = parts[0]
    for z in range(1, Z):
        total = jnp.where(lane == z, pltpu.roll(parts[z], 16 * z, 1), total)
    return total


def warp_kernel(p_ref, v_ref, l_ref, r_ref, wt_ref, st_ref, wi_ref, si_ref, wb_ref, sb_ref,
                src, c_hi, c_lo, s_hi, s_lo):
    v = pl.program_id(0)
    j, i = p_ref[180], p_ref[181]
    lane = iota((ROWS, 128), 1)
    for z in range(Z):
        q, half = z % 4, z // 4
        a, b = v_ref[0, z, :, 0:128], v_ref[0, z, :, 128:256]
        left = l_ref[:, half * 128 : half * 128 + 128]
        right = r_ref[:, half * 128 : half * 128 + 128]
        left = pltpu.roll(left, (128 - q * 24) % 128, 1) if q else left
        right = pltpu.roll(right, (128 + 24 - q * 24) % 128, 1) if q != 1 else right
        edge = jnp.where(lane < 24, left, jnp.where(lane < 48, right, jnp.where(
            lane < 64, pltpu.roll(a, 48, 1), jnp.where(lane < 80, pltpu.roll(b, 80, 1), 0.0))))
        for t, part in enumerate((a, b, edge)):
            high, low = split(part)
            src[z * 128 : z * 128 + 64, t * 128 : t * 128 + 128] = high
            src[z * 128 + 64 : z * 128 + 128, t * 128 : t * 128 + 128] = low
    src[Z * 128 :, :] = jnp.zeros((128, 384), BF16)

    def offset(axis, b, c):
        return p_ref[((v * 2 + axis) * 3 + b) * 3 + c]

    def quarter(axis, b, c):
        return p_ref[72 + ((v * 3 + axis) * 3 + b) * 3 + c].astype(F32) * 0.25

    shape = (96, 256)
    row = iota(shape, 0)
    source = iota(shape, 1)
    upper_plane = source >= 128
    source = source & 63
    target = row - 16

    def rows_matrix(c):
        def pick(values):
            return jnp.where(row < 16, values[0], jnp.where(row < 80, values[1], values[2]))

        good_c = (i > 0) if c == 0 else ((i < p_ref[183]) if c == 2 else (i >= 0))
        good = [((j > 0) & good_c).astype(F32), good_c.astype(F32), ((j < p_ref[182]) & good_c).astype(F32)]
        shift = pick([offset(1, b, c) for b in range(3)])
        f_y = pick([quarter(1, b, c) for b in range(3)])
        f_z0 = pick([(1.0 - quarter(2, b, c)) * good[b] for b in range(3)])
        f_z1 = pick([quarter(2, b, c) * good[b] for b in range(3)])
        tap = source - target - shift
        weight = jnp.where(tap == 0, 1.0 - f_y, jnp.where(tap == 1, f_y, 0.0))
        return (weight * jnp.where(upper_plane, f_z1, f_z0)).astype(BF16)

    center = rows_matrix(1)
    sides = jnp.concatenate([rows_matrix(0), rows_matrix(2)], axis=0)
    for z in range(Z):
        data = src[z * 128 : z * 128 + 256, :]
        c = jnp.dot(center, data, preferred_element_type=F32)
        s = jnp.dot(sides, data[:, 256:384], preferred_element_type=F32)
        for value, hi_ref, lo_ref, col, width in (
            (c, c_hi, c_lo, 0, 384), (s[0:96], s_hi, s_lo, 0, 128), (s[96:192], s_hi, s_lo, 128, 128)):
            high, low = split(value)
            for ref, part in ((hi_ref, high), (lo_ref, low)):
                ref[z * 64 : z * 64 + 64, col : col + width] = part[16:80]
                ref[512 + z * 16 : 528 + z * 16, col : col + width] = part[0:16]
                ref[640 + z * 16 : 656 + z * 16, col : col + width] = part[80:96]

    for b, start, count in ((1, 0, 512), (0, 512, 128), (2, 640, 128)):
        k = iota((384, COLS), 0)
        col = jnp.where(k < 256, k, jnp.where(k < 280, k - 280, jnp.where(k < 304, k - 24, 8192)))
        tap = col - iota((384, COLS), 1) - offset(0, b, 1)
        f_x = quarter(0, b, 1)
        x_map = jnp.where(tap == 0, 1.0 - f_x, jnp.where(tap == 1, f_x, 0.0)).astype(BF16)
        k = iota((256, 128), 0)
        is_right = k >= 128
        h = k & 127
        col = jnp.where(h < 24, h - 24, jnp.where(h < 48, h + 232, jnp.where(
            h < 64, h - 48, jnp.where(h < 80, h + 176, 8192))))
        out_lane = iota((256, 128), 1)
        right_lane = out_lane >= 8
        tap = col - strip_col(out_lane) - jnp.where(is_right, offset(0, b, 2), offset(0, b, 0))
        tap = jnp.where(is_right == right_lane, tap, -1)
        f_x = jnp.where(is_right, quarter(0, b, 2), quarter(0, b, 0))
        s_map = jnp.where(tap == 0, 1.0 - f_x, jnp.where(tap == 1, f_x, 0.0)).astype(BF16)
        rows = slice(start, start + count)
        w = jnp.dot(c_hi[rows], x_map, preferred_element_type=F32)
        w += jnp.dot(c_lo[rows], x_map, preferred_element_type=F32)
        s = jnp.dot(s_hi[rows], s_map, preferred_element_type=F32)
        s += jnp.dot(s_lo[rows], s_map, preferred_element_type=F32)
        count = count // Z
        if b == 1:
            places = [(wt_ref, st_ref, 16, 0, 16), (wi_ref, si_ref, 0, 16, 48), (wb_ref, sb_ref, 0, 48, 64)]
        else:
            places = [(wt_ref, st_ref, 0, 0, 16) if b == 0 else (wb_ref, sb_ref, 16, 0, 16)]
        for w_ref, s_ref, at, first, last in places:
            to = slice(at, at + last - first)
            for z in range(Z):
                w_ref[0, z, to] = w[z * count + first : z * count + last]
            s_ref[0, to] = planes_to_lanes([s[z * count + first : z * count + last] for z in range(Z)])


def warp(params, views, left, right):
    w = jax.ShapeDtypeStruct((VIEWS, Z, SET, COLS), F32)
    s = jax.ShapeDtypeStruct((VIEWS, SET, 128), F32)
    w_spec = pl.BlockSpec((1, Z, SET, COLS), lambda v: (v, 0, 0, 0))
    s_spec = pl.BlockSpec((1, SET, 128), lambda v: (v, 0, 0))
    side = pl.BlockSpec((ROWS, COLS), lambda v: (v, 0))
    return pl.pallas_call(
        warp_kernel,
        grid=(VIEWS,),
        out_shape=[w, s] * 3,
        in_specs=[SMEM, pl.BlockSpec((1, Z, ROWS, COLS), lambda v: (v, 0, 0, 0)), side, side],
        out_specs=[w_spec, s_spec] * 3,
        scratch_shapes=[
            pltpu.VMEM((9 * 128, 384), BF16),
            pltpu.VMEM((768, 384), BF16),
            pltpu.VMEM((768, 384), BF16),
            pltpu.VMEM((768, 256), BF16),
            pltpu.VMEM((768, 256), BF16),
        ],
        name="warp",
        compiler_params=limit(20),
        cost_estimate=pl.CostEstimate(flops=6_000_000_000, bytes_accessed=8_000_000, transcendentals=0),
    )(params, views, left, right)


def main_kernel(mode, *refs):
    refs = list(refs)
    k_ref, e_ref, sides_ref = refs[:3]
    refs = refs[3:]
    if mode != "inner":
        halo, refs = refs[0], refs[1:]
    w_ref, s_ref, ly, f_hi, f_lo, f_t, f_s, b_hi, b_lo, b_t, m_ref, n_ref = refs[:12]
    refs = refs[12:]
    outs = 1 if mode == "inner" else 2
    out_refs, refs = refs[:outs], refs[outs:]
    d, g_hi, g_lo, g_t, cen, q_hi, q_lo, q_t, x2 = refs
    lane = iota((NEAR, 128), 1)
    lane_out = iota((VIEWS * SET, 128), 1)
    for z in range(Z):
        edge = slice(z * EDGE, (z + 1) * EDGE)
        tail = slice(Z * EDGE, (Z + 1) * EDGE)

        def rows(own, beside):
            if mode == "inner":
                return own(8, 56)
            if mode == "top":
                return jnp.concatenate([beside, own(0, EDGE)], axis=0)
            return jnp.concatenate([own(ROWS - EDGE, ROWS), beside], axis=0)

        def both_of(cols):
            near = rows(lambda a, b: e_ref[z, a:b, cols], None if mode == "inner" else halo[edge, cols])
            far = rows(lambda a, b: sides_ref[a:b, cols], None if mode == "inner" else halo[tail, cols])
            return near, far

        c0, lh = both_of(slice(0, 128))
        c1, rh = both_of(slice(128, 256))
        lh = pltpu.roll(lh, (128 - z * 16) % 128, 1) if z else lh
        rh = pltpu.roll(rh, (128 + 16 - z * 16) % 128, 1) if z != 1 else rh
        h = jnp.where(lane < 16, lh, jnp.where(lane < 32, rh, jnp.where(
            lane < 40, pltpu.roll(c0, 32, 1), jnp.where(lane < 48, pltpu.roll(c1, 48, 1), 0.0))))
        h = jnp.where(lane < 48, h, jnp.where(lane < 96, pltpu.roll(h, 48, 1), 0.0))
        for t, part in enumerate((c0, c1, h)):
            high, low = split(part)
            cols = slice(t * 128, t * 128 + 128)
            d[0:NEAR, cols] = high
            d[NEAR : 2 * NEAR, cols] = low
            d[2 * NEAR : 3 * NEAR, cols] = high
        y = jnp.dot(ly[...], d[...], preferred_element_type=F32)
        high = y.astype(BF16)
        low = y - high.astype(F32)
        both = jnp.where(lane_out < 48, y[:, 256:384], low[:, 256:384]).astype(BF16)
        low = low.astype(BF16)
        for v in range(VIEWS):
            to, at = slice(z * SET, (z + 1) * SET), slice(v * SET, (v + 1) * SET)
            g_hi[v, to, :] = high[at, 0:256]
            g_lo[v, to, :] = low[at, 0:256]
            g_t[v, to, 0:128] = both[at]
            g_t[v, to, 128:256] = high[at, 256:384]

    def dot(a, b):
        return jnp.dot(a, b, preferred_element_type=F32)

    plane = iota((SET, 128), 1) // 16
    lanes = iota((SET, 128), 1)

    def turn(value, by):
        return pltpu.roll(value, by % 128, 1) if by % 128 else value

    for v in range(VIEWS):
        cen[v] = (dot(g_hi[v], f_hi[v]) + dot(g_lo[v], f_hi[v])) + (
            dot(g_hi[v], f_lo[v]) + dot(g_t[v], f_t[v]))
        strip = dot(g_t[v], f_s[v])
        taps = [k_ref[2 * VIEWS * TAPS + v * TAPS + t] for t in range(TAPS)]
        for rb in range(SET // 16):
            for t in range(2):
                cols = slice(t * 128, t * 128 + 128)
                at = [slice(z * SET + rb * 16, z * SET + rb * 16 + 16) for z in range(Z)]
                f = [cen[v, at[z], cols] for z in range(Z)]
                ratio = []
                for z in range(Z):
                    total = taps[7 - z] * f[0]
                    for y in range(1, Z):
                        total = total + taps[y - z + 7] * f[y]
                    total = jnp.where(total == 0.0, 1.0, total)
                    ratio.append(w_ref[v, z, rb * 16 : rb * 16 + 16, cols] / total)
                for z in range(Z):
                    total = taps[z + 7] * ratio[0]
                    for y in range(1, Z):
                        total = total + taps[z - y + 7] * ratio[y]
                    high, low = split(total)
                    q_hi[v, at[z], cols] = high
                    q_lo[v, at[z], cols] = low
        strip = planes_to_lanes([strip[z * SET : (z + 1) * SET] for z in range(Z)])
        total = taps[7] * strip
        for y in range(1, Z):
            total = total + jnp.where(plane < Z - y, taps[7 + y], taps[y - 1]) * turn(strip, -16 * y)
        ratio = s_ref[v] / jnp.where(total == 0.0, 1.0, total)
        total = taps[7] * ratio
        for y in range(1, Z):
            total = total + jnp.where(plane < Z - y, taps[7 - y], taps[15 - y]) * turn(ratio, -16 * y)
        high = total.astype(BF16).astype(F32)
        low = total - high
        for z in range(Z):
            q_t[v, z * SET : (z + 1) * SET, :] = jnp.where(lanes < 16, turn(high, -16 * z), jnp.where(
                lanes < 32, turn(low, 16 - 16 * z), jnp.where(
                    lanes < 48, turn(high, 32 - 16 * z), 0.0))).astype(BF16)
        x = (dot(q_hi[v], b_hi[v]) + dot(q_lo[v], b_hi[v])) + (
            dot(q_hi[v], b_lo[v]) + dot(q_t[v], b_t[v]))
        high, low = split(x)
        for z in range(Z):
            x2[z, 0, v] = high[z * SET : (z + 1) * SET]
            x2[z, 1, v] = low[z * SET : (z + 1) * SET]
    for z in range(Z):
        high = x2[z, 0].reshape(VIEWS * SET, COLS)
        low = x2[z, 1].reshape(VIEWS * SET, COLS)
        out = jnp.dot(m_ref[...], high, preferred_element_type=F32)
        out += jnp.dot(m_ref[...], low, preferred_element_type=F32)
        out += jnp.dot(n_ref[...], high, preferred_element_type=F32)
        if mode == "inner":
            out_refs[0][z] = out
        else:
            out_refs[0][z] = out[0:EDGE]
            out_refs[1][z] = out[EDGE:NEAR]


def main(part, *args):
    rows = Z * SET
    outs = 1 if part == "inner" else 2
    return pl.pallas_call(
        functools.partial(main_kernel, part),
        out_shape=[jax.ShapeDtypeStruct((Z, NEAR // outs, COLS), F32)] * outs,
        grid=(1,),
        in_specs=[SMEM] + [VMEM] * (len(args) - 1),
        out_specs=[VMEM] * outs,
        scratch_shapes=[
            pltpu.VMEM((3 * NEAR, 384), BF16),
            pltpu.VMEM((VIEWS, rows, 256), BF16),
            pltpu.VMEM((VIEWS, rows, 256), BF16),
            pltpu.VMEM((VIEWS, rows, 256), BF16),
            pltpu.VMEM((VIEWS, rows, 256), F32),
            pltpu.VMEM((VIEWS, rows, 256), BF16),
            pltpu.VMEM((VIEWS, rows, 256), BF16),
            pltpu.VMEM((VIEWS, rows, 128), BF16),
            pltpu.VMEM((Z, 2, VIEWS, SET, COLS), BF16),
        ],
        compiler_params=limit(24),
        cost_estimate=pl.CostEstimate(flops=4_000_000_000, bytes_accessed=8_000_000, transcendentals=0),
    )(*args)


def from_before(value, axis):
    return lax.ppermute(value, axis, [(i, i + 1) for i in range(lax.axis_size(axis) - 1)])


def from_after(value, axis):
    return lax.ppermute(value, axis, [(i + 1, i) for i in range(lax.axis_size(axis) - 1)])


def neighbours(table, j, i):
    padded = jnp.pad(table, ((0, 0), (0, 0), (1, 1), (1, 1)))
    zero = jnp.int32(0)
    return lax.dynamic_slice(padded, (zero, zero, j, i), table.shape[:2] + (3, 3)).reshape(-1)


def on_device(estimate, views, psf_x, psf_y, psf_z, block_offsets, sub_shifts):
    i, j = lax.axis_index("gx"), lax.axis_index("gy")
    psf = jnp.concatenate([psf_x, psf_y, psf_z], axis=0)
    kernels = (psf / jnp.sum(psf, axis=-1, keepdims=True)).reshape(-1)
    params = jnp.concatenate(
        [neighbours(block_offsets, j, i), neighbours(sub_shifts, j, i), j[None], i[None],
         jnp.array([lax.axis_size("gy") - 1, lax.axis_size("gx") - 1], jnp.int32)])
    first, last = pack_edges(estimate, views)
    left, right = from_before(last, "gx"), from_after(first, "gx")
    ly, *x_mats, m_mat, n_mat = matrices(kernels)
    mats = (ly, *x_mats, m_mat, n_mat)
    first, last, sides = pack_rows(estimate, left, right)
    below = from_after(first, "gy")
    above = from_before(last, "gy")
    w_t, s_t, w_i, s_i, w_b, s_b = warp(params, views, left, right)
    bottom, down = main("bottom", kernels, estimate, sides, below, w_b, s_b, *mats)
    from_above = from_before(down, "gy")
    s_t, bottom, down = lax.optimization_barrier((s_t, bottom, down))
    up, top = main("top", kernels, estimate, sides, above, w_t, s_t, *mats)
    from_below = from_after(up, "gy")
    s_i, up, top = lax.optimization_barrier((s_i, up, top))
    (inner,) = main("inner", kernels, estimate, sides, w_i, s_i, *mats)

    def place(value, start):
        return jnp.pad(value, ((0, 0), (start, ROWS - start - value.shape[1]), (0, 0)))

    total = place(inner, 8) + place(top + from_above, 0) + place(bottom + from_below, ROWS - EDGE)
    return estimate * (total * 0.25)


def solution(mesh):
    in_specs = (P(None, "gy", "gx"), P(None, None, "gy", "gx"), P(), P(), P(), P(), P())
    out_specs = P(None, "gy", "gx")
    return jax.shard_map(
        on_device, mesh=mesh, in_specs=in_specs, out_specs=out_specs, check_vma=False
    )
```

```python
import functools

import jax
import jax.numpy as jnp
from jax import lax
from jax.experimental import pallas as pl
from jax.experimental.pallas import tpu as pltpu
from jax.sharding import PartitionSpec as P


F32 = jnp.float32
BF16 = jnp.bfloat16
VIEWS = 4
TAPS = 15
Z = 8
ROWS = 64
COLS = 256
SET = 32
NEAR = 48
EDGE = 24

SMEM = pl.BlockSpec(memory_space=pltpu.SMEM)
VMEM = pl.BlockSpec(memory_space=pltpu.VMEM)


def limit(mib):
    return pltpu.CompilerParams(vmem_limit_bytes=mib << 20)


def iota(shape, dim):
    return lax.broadcasted_iota(jnp.int32, shape, dim)


def strip_col(lane):
    return jnp.where(lane < 8, lane - 8, jnp.where(lane < 16, lane + 248, 4096))


def roll(value, by):
    return pltpu.roll(value, by % 128, 1) if by % 128 else value


def split(value):
    high = value.astype(BF16)
    return high, (value - high.astype(F32)).astype(BF16)


def band(k_ref, base, differ):
    total = jnp.zeros(differ.shape, F32)
    for tap in range(TAPS):
        total = jnp.where(differ == tap, k_ref[base + tap], total)
    return total


def matrices_kernel(k_ref, ly, f_hi, f_lo, f_t, f_s, b_hi, b_lo, b_t, m_ref, n_ref):
    kx, ky = 0, VIEWS * TAPS
    shape = (SET, 3 * NEAR)
    lane = iota(shape, 1)
    seg = jnp.where(lane < NEAR, 0, jnp.where(lane < 2 * NEAR, 1, 2))
    differ = lane - seg * NEAR - iota(shape, 0) - 1
    for v in range(VIEWS):
        weight = band(k_ref, ky + v * TAPS, differ)
        high = weight.astype(BF16).astype(F32)
        ly[v * SET : (v + 1) * SET, :] = jnp.where(seg < 2, high, weight - high).astype(BF16)

    view = iota((1, VIEWS * SET), 1) // SET
    taps = []
    for tap in range(TAPS):
        value = jnp.full(view.shape, k_ref[ky + tap])
        for v in range(1, VIEWS):
            value = jnp.where(view == v, k_ref[ky + v * TAPS + tap], value)
        taps.append(value)
    shape = (NEAR, VIEWS * SET)
    differ = iota(shape, 0) - (iota(shape, 1) & (SET - 1)) - 1
    weight = jnp.zeros(shape, F32)
    for tap in range(TAPS):
        weight = jnp.where(differ == tap, taps[tap], weight)
    high, low = split(weight)
    m_ref[...] = high
    n_ref[...] = low

    def per_view(v, carry):
        base = kx + v * TAPS
        differ = iota((128, 128), 0) - iota((128, 128), 1) + 7
        corner = iota((16, 128), 0) - iota((16, 128), 1)
        for mirrored, hi_ref, lo_ref in ((False, f_hi, f_lo), (True, b_hi, b_lo)):
            def parts(d):
                return split(band(k_ref, base, 14 - d if mirrored else d))

            diagonal, lower, upper = parts(differ), parts(corner + 135), parts(corner - 9)
            for ref, a, b, c in zip((hi_ref, lo_ref), diagonal, lower, upper):
                ref[v, 0:128, 0:128] = a
                ref[v, 128:256, 128:256] = a
                ref[v, 128:144, 0:128] = b
                ref[v, 144:256, 0:128] = jnp.zeros((112, 128), BF16)
                ref[v, 112:128, 128:256] = c
                ref[v, 0:112, 128:256] = jnp.zeros((112, 128), BF16)
        for out_ref, width in ((f_t, COLS), (f_s, 128)):
            shape = (48, width)
            place = iota(shape, 0)
            source = jnp.where(
                place < 16,
                place - 16,
                jnp.where(place < 32, place + 240, jnp.where(place < 40, place - 32, place + 208)),
            )
            target = iota(shape, 1) if width == COLS else strip_col(iota(shape, 1))
            differ = source - target + 7
            if width == COLS:
                differ = jnp.where(place < 32, differ, -1)
            high, low = split(band(k_ref, base, differ))
            out_ref[v, 0:48] = high
            out_ref[v, 48:96] = high
            out_ref[v, 96:128] = jnp.zeros((32, width), BF16)
            out_ref[v, 128:176] = low
            out_ref[v, 176:256] = jnp.zeros((80, width), BF16)
        shape = (16, COLS)
        high, low = split(band(k_ref, base, iota(shape, 1) - strip_col(iota(shape, 0)) + 7))
        b_t[v, 0:16] = high
        b_t[v, 16:32] = high
        b_t[v, 32:48] = low
        b_t[v, 48:128] = jnp.zeros((80, COLS), BF16)
        return carry

    lax.fori_loop(0, VIEWS, per_view, 0)


def matrices(kernels):
    shapes = [
        (128, 144), (4, 256, 256), (4, 256, 256), (4, 256, 256), (4, 256, 128),
        (4, 256, 256), (4, 256, 256), (4, 128, 256), (48, 128), (48, 128),
    ]
    return pl.pallas_call(
        matrices_kernel,
        out_shape=[jax.ShapeDtypeStruct(s, BF16) for s in shapes],
        in_specs=[SMEM],
        out_specs=[VMEM] * len(shapes),
        name="matrices",
        compiler_params=limit(12),
        cost_estimate=pl.CostEstimate(flops=8_000_000, bytes_accessed=4_000_000, transcendentals=0),
    )(kernels)


def pack_edges_kernel(e_ref, v_ref, left_ref, right_ref):
    lane = iota((ROWS, 128), 1)
    for half in range(2):
        left = jnp.zeros((ROWS, 128), F32)
        right = jnp.zeros((ROWS, 128), F32)
        pieces = [(v_ref[0, half * 4 + q], q * 24, 24) for q in range(4)]
        if half == 0:
            pieces += [(e_ref[q], 96 + q * 16, 16) for q in range(2)]
        for plane, at, width in pieces:
            inside = (lane >= at) & (lane < at + width)
            left = jnp.where(inside, roll(plane[:, 0:128], at), left)
            right = jnp.where(inside, roll(plane[:, 128:256], at + width), right)
        left_ref[:, half * 128 : half * 128 + 128] = left
        right_ref[:, half * 128 : half * 128 + 128] = right


def pack_edges(estimate, views):
    out = jax.ShapeDtypeStruct((VIEWS * ROWS, COLS), F32)
    spec = pl.BlockSpec((ROWS, COLS), lambda v: (v, 0))
    return pl.pallas_call(
        pack_edges_kernel,
        grid=(VIEWS,),
        out_shape=[out, out],
        in_specs=[
            pl.BlockSpec((2, ROWS, COLS), lambda v: (v, 0, 0)),
            pl.BlockSpec((1, Z, ROWS, COLS), lambda v: (v, 0, 0, 0)),
        ],
        out_specs=[spec, spec],
        name="pack_edges",
        compiler_params=limit(12),
        cost_estimate=pl.CostEstimate(flops=1_000_000, bytes_accessed=3_200_000, transcendentals=0),
    )(estimate, views)


def pack_rows_kernel(e_ref, l_ref, r_ref, first_ref, last_ref, sides_ref):
    lane = iota((ROWS, 128), 1) // 32
    for ref, cols in ((l_ref, slice(0, 128)), (r_ref, slice(128, 256))):
        side = roll(ref[0:ROWS, 0:128], -96)
        for v in range(1, VIEWS):
            part = roll(ref[v * ROWS : (v + 1) * ROWS, 0:128], 32 * v - 96)
            side = jnp.where(lane == v, part, side)
        sides_ref[:, cols] = side
        first_ref[Z * EDGE :, cols] = side[0:EDGE]
        last_ref[Z * EDGE :, cols] = side[ROWS - EDGE :]
    for out_ref, start in ((first_ref, 0), (last_ref, ROWS - EDGE)):
        for z in range(Z):
            out_ref[z * EDGE : (z + 1) * EDGE, :] = e_ref[z, start : start + EDGE, :]


def pack_rows(estimate, left, right):
    rows = jax.ShapeDtypeStruct(((Z + 1) * EDGE, COLS), F32)
    return pl.pallas_call(
        pack_rows_kernel,
        out_shape=[rows, rows, jax.ShapeDtypeStruct((ROWS, COLS), F32)],
        in_specs=[VMEM] * 3,
        out_specs=[VMEM] * 3,
        name="pack_rows",
        compiler_params=limit(12),
    )(estimate, left, right)


def planes_to_lanes(parts):
    lane = iota(parts[0].shape, 1) // 16
    total = parts[0]
    for z in range(1, Z):
        total = jnp.where(lane == z, pltpu.roll(parts[z], 16 * z, 1), total)
    return total


def warp_kernel(p_ref, v_ref, l_ref, r_ref, wt_ref, st_ref, wi_ref, si_ref, wb_ref, sb_ref,
                src, c_hi, c_lo, s_hi, s_lo):
    v = pl.program_id(0)
    j, i = p_ref[180], p_ref[181]
    lane = iota((ROWS, 128), 1)
    for z in range(Z):
        q, half = z % 4, z // 4
        a, b = v_ref[0, z, :, 0:128], v_ref[0, z, :, 128:256]
        left = l_ref[:, half * 128 : half * 128 + 128]
        right = r_ref[:, half * 128 : half * 128 + 128]
        left = pltpu.roll(left, (128 - q * 24) % 128, 1) if q else left
        right = pltpu.roll(right, (128 + 24 - q * 24) % 128, 1) if q != 1 else right
        edge = jnp.where(lane < 24, left, jnp.where(lane < 48, right, jnp.where(
            lane < 64, pltpu.roll(a, 48, 1), jnp.where(lane < 80, pltpu.roll(b, 80, 1), 0.0))))
        for t, part in enumerate((a, b, edge)):
            high, low = split(part)
            src[z * 128 : z * 128 + 64, t * 128 : t * 128 + 128] = high
            src[z * 128 + 64 : z * 128 + 128, t * 128 : t * 128 + 128] = low
    src[Z * 128 :, :] = jnp.zeros((128, 384), BF16)

    def offset(axis, b, c):
        return p_ref[((v * 2 + axis) * 3 + b) * 3 + c]

    def quarter(axis, b, c):
        return p_ref[72 + ((v * 3 + axis) * 3 + b) * 3 + c].astype(F32) * 0.25

    shape = (96, 256)
    row = iota(shape, 0)
    source = iota(shape, 1)
    upper_plane = source >= 128
    source = source & 63
    target = row - 16

    def rows_matrix(c):
        def pick(values):
            return jnp.where(row < 16, values[0], jnp.where(row < 80, values[1], values[2]))

        good_c = (i > 0) if c == 0 else ((i < p_ref[183]) if c == 2 else (i >= 0))
        good = [((j > 0) & good_c).astype(F32), good_c.astype(F32), ((j < p_ref[182]) & good_c).astype(F32)]
        shift = pick([offset(1, b, c) for b in range(3)])
        f_y = pick([quarter(1, b, c) for b in range(3)])
        f_z0 = pick([(1.0 - quarter(2, b, c)) * good[b] for b in range(3)])
        f_z1 = pick([quarter(2, b, c) * good[b] for b in range(3)])
        tap = source - target - shift
        weight = jnp.where(tap == 0, 1.0 - f_y, jnp.where(tap == 1, f_y, 0.0))
        return (weight * jnp.where(upper_plane, f_z1, f_z0)).astype(BF16)

    center = rows_matrix(1)
    sides = jnp.concatenate([rows_matrix(0), rows_matrix(2)], axis=0)
    for z in range(Z):
        data = src[z * 128 : z * 128 + 256, :]
        c = jnp.dot(center, data, preferred_element_type=F32)
        s = jnp.dot(sides, data[:, 256:384], preferred_element_type=F32)
        for value, hi_ref, lo_ref, col, width in (
            (c, c_hi, c_lo, 0, 384), (s[0:96], s_hi, s_lo, 0, 128), (s[96:192], s_hi, s_lo, 128, 128)):
            high, low = split(value)
            for ref, part in ((hi_ref, high), (lo_ref, low)):
                ref[z * 64 : z * 64 + 64, col : col + width] = part[16:80]
                ref[512 + z * 16 : 528 + z * 16, col : col + width] = part[0:16]
                ref[640 + z * 16 : 656 + z * 16, col : col + width] = part[80:96]

    for b, start, count in ((1, 0, 512), (0, 512, 128), (2, 640, 128)):
        k = iota((384, COLS), 0)
        col = jnp.where(k < 256, k, jnp.where(k < 280, k - 280, jnp.where(k < 304, k - 24, 8192)))
        tap = col - iota((384, COLS), 1) - offset(0, b, 1)
        f_x = quarter(0, b, 1)
        x_map = jnp.where(tap == 0, 1.0 - f_x, jnp.where(tap == 1, f_x, 0.0)).astype(BF16)
        k = iota((256, 128), 0)
        is_right = k >= 128
        h = k & 127
        col = jnp.where(h < 24, h - 24, jnp.where(h < 48, h + 232, jnp.where(
            h < 64, h - 48, jnp.where(h < 80, h + 176, 8192))))
        out_lane = iota((256, 128), 1)
        right_lane = out_lane >= 8
        tap = col - strip_col(out_lane) - jnp.where(is_right, offset(0, b, 2), offset(0, b, 0))
        tap = jnp.where(is_right == right_lane, tap, -1)
        f_x = jnp.where(is_right, quarter(0, b, 2), quarter(0, b, 0))
        s_map = jnp.where(tap == 0, 1.0 - f_x, jnp.where(tap == 1, f_x, 0.0)).astype(BF16)
        rows = slice(start, start + count)
        w = jnp.dot(c_hi[rows], x_map, preferred_element_type=F32)
        w += jnp.dot(c_lo[rows], x_map, preferred_element_type=F32)
        s = jnp.dot(s_hi[rows], s_map, preferred_element_type=F32)
        s += jnp.dot(s_lo[rows], s_map, preferred_element_type=F32)
        count = count // Z
        if b == 1:
            places = [(wt_ref, st_ref, 16, 0, 16), (wi_ref, si_ref, 0, 16, 48), (wb_ref, sb_ref, 0, 48, 64)]
        else:
            places = [(wt_ref, st_ref, 0, 0, 16) if b == 0 else (wb_ref, sb_ref, 16, 0, 16)]
        for w_ref, s_ref, at, first, last in places:
            to = slice(at, at + last - first)
            for z in range(Z):
                w_ref[0, z, to] = w[z * count + first : z * count + last]
            s_ref[0, to] = planes_to_lanes([s[z * count + first : z * count + last] for z in range(Z)])


def warp(params, views, left, right):
    w = jax.ShapeDtypeStruct((VIEWS, Z, SET, COLS), F32)
    s = jax.ShapeDtypeStruct((VIEWS, SET, 128), F32)
    w_spec = pl.BlockSpec((1, Z, SET, COLS), lambda v: (v, 0, 0, 0))
    s_spec = pl.BlockSpec((1, SET, 128), lambda v: (v, 0, 0))
    side = pl.BlockSpec((ROWS, COLS), lambda v: (v, 0))
    return pl.pallas_call(
        warp_kernel,
        grid=(VIEWS,),
        out_shape=[w, s] * 3,
        in_specs=[SMEM, pl.BlockSpec((1, Z, ROWS, COLS), lambda v: (v, 0, 0, 0)), side, side],
        out_specs=[w_spec, s_spec] * 3,
        scratch_shapes=[
            pltpu.VMEM((9 * 128, 384), BF16),
            pltpu.VMEM((768, 384), BF16),
            pltpu.VMEM((768, 384), BF16),
            pltpu.VMEM((768, 256), BF16),
            pltpu.VMEM((768, 256), BF16),
        ],
        name="warp",
        compiler_params=limit(20),
        cost_estimate=pl.CostEstimate(flops=6_000_000_000, bytes_accessed=8_000_000, transcendentals=0),
    )(params, views, left, right)


def main_kernel(mode, *refs):
    refs = list(refs)
    k_ref, e_ref, sides_ref = refs[:3]
    refs = refs[3:]
    if mode != "inner":
        halo, refs = refs[0], refs[1:]
    w_ref, s_ref, ly, f_hi, f_lo, f_t, f_s, b_hi, b_lo, b_t, m_ref, n_ref = refs[:12]
    refs = refs[12:]
    outs = 1 if mode == "inner" else 2
    out_refs, refs = refs[:outs], refs[outs:]
    d, g_hi, g_lo, g_t, cen, q_t, x2 = refs
    lane = iota((NEAR, 128), 1)
    lane_out = iota((VIEWS * SET, 128), 1)
    for z in range(Z):
        edge = slice(z * EDGE, (z + 1) * EDGE)
        tail = slice(Z * EDGE, (Z + 1) * EDGE)

        def rows(own, beside):
            if mode == "inner":
                return own(8, 56)
            if mode == "top":
                return jnp.concatenate([beside, own(0, EDGE)], axis=0)
            return jnp.concatenate([own(ROWS - EDGE, ROWS), beside], axis=0)

        def both_of(cols):
            near = rows(lambda a, b: e_ref[z, a:b, cols], None if mode == "inner" else halo[edge, cols])
            far = rows(lambda a, b: sides_ref[a:b, cols], None if mode == "inner" else halo[tail, cols])
            return near, far

        c0, lh = both_of(slice(0, 128))
        c1, rh = both_of(slice(128, 256))
        lh = pltpu.roll(lh, (128 - z * 16) % 128, 1) if z else lh
        rh = pltpu.roll(rh, (128 + 16 - z * 16) % 128, 1) if z != 1 else rh
        h = jnp.where(lane < 16, lh, jnp.where(lane < 32, rh, jnp.where(
            lane < 40, pltpu.roll(c0, 32, 1), jnp.where(lane < 48, pltpu.roll(c1, 48, 1), 0.0))))
        h = jnp.where(lane < 48, h, jnp.where(lane < 96, pltpu.roll(h, 48, 1), 0.0))
        for t, part in enumerate((c0, c1, h)):
            high, low = split(part)
            cols = slice(t * 128, t * 128 + 128)
            d[0:NEAR, cols] = high
            d[NEAR : 2 * NEAR, cols] = low
            d[2 * NEAR : 3 * NEAR, cols] = high
        y = jnp.dot(ly[...], d[...], preferred_element_type=F32)
        high = y.astype(BF16)
        low = y - high.astype(F32)
        both = jnp.where(lane_out < 48, y[:, 256:384], low[:, 256:384]).astype(BF16)
        low = low.astype(BF16)
        for v in range(VIEWS):
            to, at = slice(z * SET, (z + 1) * SET), slice(v * SET, (v + 1) * SET)
            g_hi[v, to, :] = high[at, 0:256]
            g_lo[v, to, :] = low[at, 0:256]
            g_t[v, to, 0:128] = both[at]
            g_t[v, to, 128:256] = high[at, 256:384]

    def dot(a, b):
        return jnp.dot(a, b, preferred_element_type=F32)

    plane = iota((SET, 128), 1) // 16
    lanes = iota((SET, 128), 1)

    def turn(value, by):
        return pltpu.roll(value, by % 128, 1) if by % 128 else value

    for v in range(VIEWS):
        cen[v] = (dot(g_hi[v], f_hi[v]) + dot(g_lo[v], f_hi[v])) + (
            dot(g_hi[v], f_lo[v]) + dot(g_t[v], f_t[v]))
        strip = dot(g_t[v], f_s[v])
        taps = [k_ref[2 * VIEWS * TAPS + v * TAPS + t] for t in range(TAPS)]
        for rb in range(SET // 8):
            for t in range(2):
                cols = slice(t * 128, t * 128 + 128)
                at = [slice(z * SET + rb * 8, z * SET + rb * 8 + 8) for z in range(Z)]
                f = [cen[v, at[z], cols] for z in range(Z)]
                ratio = []
                for z in range(Z):
                    total = taps[7 - z] * f[0]
                    for y in range(1, Z):
                        total = total + taps[y - z + 7] * f[y]
                    total = jnp.where(total == 0.0, 1.0, total)
                    ratio.append(w_ref[v, z, rb * 8 : rb * 8 + 8, cols] / total)
                for z in range(Z):
                    total = taps[z + 7] * ratio[0]
                    for y in range(1, Z):
                        total = total + taps[z - y + 7] * ratio[y]
                    cen[v, at[z], cols] = total
        strip = planes_to_lanes([strip[z * SET : (z + 1) * SET] for z in range(Z)])
        total = taps[7] * strip
        for y in range(1, Z):
            total = total + jnp.where(plane < Z - y, taps[7 + y], taps[y - 1]) * turn(strip, -16 * y)
        ratio = s_ref[v] / jnp.where(total == 0.0, 1.0, total)
        total = taps[7] * ratio
        for y in range(1, Z):
            total = total + jnp.where(plane < Z - y, taps[7 - y], taps[15 - y]) * turn(ratio, -16 * y)
        high = total.astype(BF16).astype(F32)
        low = total - high
        for z in range(Z):
            q_t[v, z * SET : (z + 1) * SET, :] = jnp.where(lanes < 16, turn(high, -16 * z), jnp.where(
                lanes < 32, turn(low, 16 - 16 * z), jnp.where(
                    lanes < 48, turn(high, 32 - 16 * z), 0.0))).astype(BF16)
        q_hi, q_lo = split(cen[v])
        x = (dot(q_hi, b_hi[v]) + dot(q_lo, b_hi[v])) + (
            dot(q_hi, b_lo[v]) + dot(q_t[v], b_t[v]))
        high, low = split(x)
        for z in range(Z):
            x2[z, 0, v] = high[z * SET : (z + 1) * SET]
            x2[z, 1, v] = low[z * SET : (z + 1) * SET]
    for z in range(Z):
        high = x2[z, 0].reshape(VIEWS * SET, COLS)
        low = x2[z, 1].reshape(VIEWS * SET, COLS)
        out = jnp.dot(m_ref[...], high, preferred_element_type=F32)
        out += jnp.dot(m_ref[...], low, preferred_element_type=F32)
        out += jnp.dot(n_ref[...], high, preferred_element_type=F32)
        if mode == "inner":
            out_refs[0][z] = out
        else:
            out_refs[0][z] = out[0:EDGE]
            out_refs[1][z] = out[EDGE:NEAR]


def main(part, *args):
    rows = Z * SET
    outs = 1 if part == "inner" else 2
    return pl.pallas_call(
        functools.partial(main_kernel, part),
        out_shape=[jax.ShapeDtypeStruct((Z, NEAR // outs, COLS), F32)] * outs,
        grid=(1,),
        in_specs=[SMEM] + [VMEM] * (len(args) - 1),
        out_specs=[VMEM] * outs,
        scratch_shapes=[
            pltpu.VMEM((3 * NEAR, 384), BF16),
            pltpu.VMEM((VIEWS, rows, 256), BF16),
            pltpu.VMEM((VIEWS, rows, 256), BF16),
            pltpu.VMEM((VIEWS, rows, 256), BF16),
            pltpu.VMEM((VIEWS, rows, 256), F32),
            pltpu.VMEM((VIEWS, rows, 128), BF16),
            pltpu.VMEM((Z, 2, VIEWS, SET, COLS), BF16),
        ],
        compiler_params=limit(24),
        cost_estimate=pl.CostEstimate(flops=4_000_000_000, bytes_accessed=8_000_000, transcendentals=0),
    )(*args)


def from_before(value, axis):
    return lax.ppermute(value, axis, [(i, i + 1) for i in range(lax.axis_size(axis) - 1)])


def from_after(value, axis):
    return lax.ppermute(value, axis, [(i + 1, i) for i in range(lax.axis_size(axis) - 1)])


def neighbours(table, j, i):
    padded = jnp.pad(table, ((0, 0), (0, 0), (1, 1), (1, 1)))
    zero = jnp.int32(0)
    return lax.dynamic_slice(padded, (zero, zero, j, i), table.shape[:2] + (3, 3)).reshape(-1)


def on_device(estimate, views, psf_x, psf_y, psf_z, block_offsets, sub_shifts):
    i, j = lax.axis_index("gx"), lax.axis_index("gy")
    psf = jnp.concatenate([psf_x, psf_y, psf_z], axis=0)
    kernels = (psf / jnp.sum(psf, axis=-1, keepdims=True)).reshape(-1)
    params = jnp.concatenate(
        [neighbours(block_offsets, j, i), neighbours(sub_shifts, j, i), j[None], i[None],
         jnp.array([lax.axis_size("gy") - 1, lax.axis_size("gx") - 1], jnp.int32)])
    first, last = pack_edges(*(pltpu.with_memory_space_constraint(a, pltpu.HBM) for a in (estimate, views)))
    left, right = from_before(last, "gx"), from_after(first, "gx")
    ly, *x_mats, m_mat, n_mat = matrices(kernels)
    mats = (ly, *x_mats, m_mat, n_mat)
    first, last, sides = pack_rows(estimate, left, right)
    below = from_after(first, "gy")
    w_t, s_t, w_i, s_i, w_b, s_b = warp(params, views, left, right)
    last, s_t = lax.optimization_barrier((last, s_t))
    above = from_before(last, "gy")
    bottom, down = main("bottom", kernels, estimate, sides, below, w_b, s_b, *mats)
    from_above = from_before(down, "gy")
    s_t, bottom, down = lax.optimization_barrier((s_t, bottom, down))
    up, top = main("top", kernels, estimate, sides, above, w_t, s_t, *mats)
    from_below = from_after(up, "gy")
    s_i, up, top = lax.optimization_barrier((s_i, up, top))
    (inner,) = main("inner", kernels, estimate, sides, w_i, s_i, *mats)

    def place(value, start):
        return jnp.pad(value, ((0, 0), (start, ROWS - start - value.shape[1]), (0, 0)))

    total = place(inner, 8) + place(top + from_above, 0) + place(bottom + from_below, ROWS - EDGE)
    return estimate * (total * 0.25)


def solution(mesh):
    in_specs = (P(None, "gy", "gx"), P(None, None, "gy", "gx"), P(), P(), P(), P(), P())
    out_specs = P(None, "gy", "gx")
    return jax.shard_map(
        on_device, mesh=mesh, in_specs=in_specs, out_specs=out_specs, check_vma=False
    )
```
